128 devices in a mesh: segment: 4 (over y), dp: 32 (over z, x, core).
Axes of the slice: x: 4, y: 4, z: 4, core: 2. Of those that a mesh axis runs over, the one named last changes fastest.
Arguments:
- video_clips: bfloat16 [32, 9, 192, 128], P('dp'), may hold values from -6 to 6
- conv_weight: bfloat16 [4, 192, 5184], P('segment'), may hold values from -0.078125 to 0.078125
- norm_gain: float32 [4, 192], P('segment'), may hold values from 0.1 to 1.9
- cotangent: bfloat16 [32, 9, 192, 128], P('dp'), may hold values from -12 to 12
- clip_groups: int32 [32], P('dp'), may hold values from 1 to 3, as said below
Outputs:
- section_features: bfloat16 [4, 32, 9, 192, 128], P('segment', 'dp')
- grad_weight: float32 [4, 192, 5184], P('segment', 'dp')
- grad_gain: float32 [4, 192], P('segment', 'dp')
The draws below stay inside these ranges and needn't reach their ends.
Inputs may be any that keep to these rules, and one draw needn't show every extreme that they name: `clip_groups`: A clip of k groups has 4 * k - 3 frames; later frames are not part of it. Some clip has 3 groups.
All inputs are finite; a program needn't handle non-finite values.
Results may differ from the reference program's by a relative error of at most 0.0095.
Values may be sent and summed in bfloat16 or wider, within the bound.
A program may use at most 128 MiB of HBM per device.

```python
import jax
import jax.numpy as jnp
from jax import lax

C = 192
TILE_H = 8
TILE_W = 16
GROUPS = 3
FRAMES = 9
CLIPS = 32
N_SEGMENT = 4


def draw_clip_groups(key, part):
    counts = jax.random.randint(key, (CLIPS,), 1, GROUPS + 1)
    longest = jax.random.randint(jax.random.fold_in(key, 7), (), 0, CLIPS)
    return counts.at[longest].set(GROUPS).astype(jnp.int32)


def raised(entries, key, source, target, parts, factor):
    def block_of(dim):
        return (jnp.arange(entries.shape[dim]) // (entries.shape[dim] // parts)).reshape((-1,) + (1,) * (entries.ndim - 1 - dim))

    first = jax.random.permutation(key, parts)[block_of(target)]
    other_side = (block_of(target) + parts // 2) % parts
    return jnp.where((block_of(source) == first) | (block_of(source) == other_side), factor * entries, entries)


def block_scale(rng, shape, pieces, least, high):
    loudness, own = 1.0, jax.random.fold_in(rng, 6)
    for dim, shards_of in pieces:
        draws = jnp.exp(jax.random.uniform(jax.random.fold_in(own, dim), (shards_of,), jnp.float32, least / len(pieces), high / len(pieces)))
        loudness = loudness * jnp.repeat(draws, shape[dim] // shards_of).reshape([-1 if axis == dim else 1 for axis in range(len(shape))])
    return loudness


def gaussian(key, extent, width, limit, split=(), kind=jnp.bfloat16):
    drawn = width * jax.random.normal(key, extent, jnp.float32)
    if split:
        drawn = drawn * block_scale(key, extent, split, -0.22, 0.18)
    return jnp.clip(drawn, -limit, limit).astype(kind)


def bell_draw_with(stream_key, shape, width, reach, shards, heavy, kind=jnp.bfloat16):
    values = width * jax.random.normal(stream_key, shape, jnp.float32)
    if shards:
        values = values * block_scale(stream_key, shape, shards, -0.22, 0.18)
    return jnp.clip(raised(values, jax.random.fold_in(stream_key, 3), *heavy), -reach, reach).astype(kind)


def setup_inputs(seed: int = 0) -> dict:
    streams_of = jax.random.split(jax.random.key(seed), 6)
    video_clips = gaussian(streams_of[0], (CLIPS, FRAMES, C, TILE_H * TILE_W), 1.0, 6.0, ((0, 32),))
    conv_weight = gaussian(streams_of[1], (N_SEGMENT, C, 27 * C), (27 * C) ** -0.5, 0.078125, ((0, 4),))
    norm_gain = jnp.clip(1.0 + 0.18 * jax.random.normal(streams_of[2], (N_SEGMENT, C), jnp.float32), 0.1, 1.9)
    cotangent = bell_draw_with(streams_of[3], (CLIPS, FRAMES, C, TILE_H * TILE_W), 1.0, 12.0, ((0, 32),), (0, 2, 32, 2.75))
    clip_groups = draw_clip_groups(jax.random.fold_in(streams_of[5], 71), 0)
    return dict(video_clips=video_clips, conv_weight=conv_weight, norm_gain=norm_gain, cotangent=cotangent, clip_groups=clip_groups)


epsilon = 1e-06

def normalize(values, gain_vec):
    scale = lax.rsqrt(lax.optimization_barrier(jnp.mean(values * values, axis=1, keepdims=True)) + epsilon)
    return values * scale * gain_vec[None, :, None]

def make_patches(normed):
    frames = normed.shape[0]
    blocks = frames - 2
    channels = normed.shape[1]
    positions = normed.shape[2]
    grid = normed.reshape(frames, channels, TILE_H, TILE_W)
    padded = jnp.pad(grid, ((0, 0), (0, 0), (1, 1), (1, 1)))
    spatial = jnp.stack([padded[:, :, row:row + TILE_H, col:col + TILE_W].reshape(frames, channels, positions) for row in range(3) for col in range(3)], axis=1)
    stacked = jnp.concatenate([spatial[tap:tap + blocks] for tap in range(3)], axis=1)
    return stacked.reshape(blocks, 27 * channels, positions)

def section_forward(window, kernel, gain_vec, frame_mask):
    normed = normalize(window.astype(jnp.float32), gain_vec).astype(jnp.bfloat16)
    patches = make_patches(normed)
    conv = jnp.einsum('ok,fkp->fop', kernel.astype(jnp.float32), patches.astype(jnp.float32))
    return ((window[2:].astype(jnp.float32) + jax.nn.silu(conv)) * frame_mask[:, None, None]).astype(jnp.bfloat16)

def section_backward(window, kernel, gain_vec, frame_mask, upstream):
    as_float = window.astype(jnp.float32)
    normed_float, norm_back = jax.vjp(normalize, as_float, gain_vec)
    normed = normed_float.astype(jnp.bfloat16)
    patches = make_patches(normed)
    conv = jnp.einsum('ok,fkp->fop', kernel.astype(jnp.float32), patches.astype(jnp.float32))
    grad_z = upstream.astype(jnp.float32) * frame_mask[:, None, None]
    sigmoid = jax.nn.sigmoid(conv)
    grad_conv = (grad_z * sigmoid * (1.0 + conv * (1.0 - sigmoid))).astype(jnp.bfloat16)
    weight_part = jnp.einsum('fop,fkp->ok', grad_conv.astype(jnp.float32), patches.astype(jnp.float32))
    grad_patch = jnp.einsum('ok,fop->fkp', kernel.astype(jnp.float32), grad_conv.astype(jnp.float32))
    unused, patch_back = jax.vjp(make_patches, jnp.zeros(window.shape, jnp.float32))
    grad_normed = patch_back(grad_patch)[0]
    window_grad, gain_part = norm_back(grad_normed)
    window_grad = window_grad.at[2:].add(grad_z)
    return (window_grad, weight_part, gain_part)

def reference(video_clips, conv_weight, norm_gain, cotangent, clip_groups):
    positions = TILE_H * TILE_W
    padded_len = FRAMES + 3
    places = jnp.arange(padded_len, dtype=jnp.int32)

    def one_clip(carried, item):
        clip_frames, clip_grad, group_count = item
        frame_mask = ((places >= 3) & (places < 4 * group_count)).astype(jnp.float32)
        masked = clip_frames * frame_mask[3:, None, None].astype(jnp.bfloat16)
        current = jnp.concatenate([jnp.zeros((5, C, positions), jnp.bfloat16), masked])
        held_inputs = []
        outputs = []
        for section in range(N_SEGMENT):
            held_inputs.append(current)
            result = section_forward(current, conv_weight[section], norm_gain[section], frame_mask)
            outputs.append(result[3:])
            current = jnp.concatenate([jnp.zeros((2, C, positions), jnp.bfloat16), result])
        upstream = jnp.concatenate([jnp.zeros((3, C, positions), jnp.float32), clip_grad.astype(jnp.float32)])
        weight_parts = [None] * N_SEGMENT
        gain_parts = [None] * N_SEGMENT
        for section in reversed(range(N_SEGMENT)):
            window_grad, weight_part, gain_part = section_backward(held_inputs[section], conv_weight[section], norm_gain[section], frame_mask, upstream)
            weight_parts[section] = weight_part
            gain_parts[section] = gain_part
            upstream = window_grad[2:]
        carried = (carried[0] + jnp.stack(weight_parts), carried[1] + jnp.stack(gain_parts))
        return (carried, jnp.stack(outputs))
    initial = (jnp.zeros((N_SEGMENT, C, 27 * C), jnp.float32), jnp.zeros((N_SEGMENT, C), jnp.float32))
    sums, features = lax.scan(one_clip, initial, (video_clips, cotangent, clip_groups))
    return (jnp.transpose(features, (1, 0, 2, 3, 4)), sums[0], sums[1])
```

```python
import jax
import jax.numpy as jnp
from jax import lax
from jax.experimental import pallas as pl
from jax.experimental.pallas import tpu as pltpu
from jax.sharding import PartitionSpec as P

TILE_H = 8
TILE_W = 16
EPS = 1e-06

F = 9
C = 192
PIX = 128
K3 = 9 * C
KK = 27 * C
N0 = 1408
N1 = 1280
HALF = N0 + N1

BF = jnp.bfloat16
F32 = jnp.float32
NT = (((1,), (1,)), ((), ()))


def tap_masks():
    lane = lax.broadcasted_iota(jnp.int32, (1, PIX), 1)
    col = lane & (TILE_W - 1)
    masks = []
    for a in range(3):
        for b in range(3):
            pos = lane + TILE_W * (a - 1)
            ok = (col + (b - 1) >= 0) & (col + (b - 1) < TILE_W) & (pos >= 0) & (pos < PIX)
            masks.append(jnp.where(ok, 1.0, 0.0).astype(BF))
    return masks


def store_patches(dst, base, frame):
    masks = tap_masks()
    for a in range(3):
        for b in range(3):
            k = a * 3 + b
            shift = (-(TILE_W * (a - 1) + (b - 1))) % PIX
            value = frame if shift == 0 else pltpu.roll(frame, shift, 1) * masks[k]
            dst[pl.ds(base + k * C, C), :] = value


def kernel(groups, video, weight, gain, cot, feat, dweight, dgain,
           xin, dyin, dysend, fac, scales, gain_b, gain_acc, sp, dp_, wt, dconv_all, dconv_perm,
           a0, a1, b0, b1, c0, c1, d0, d1, f0, f1, g0, g1,
           fsend, frecv, bsend, brecv, s0send, s0recv, s1send, s1recv, s2send, s2recv):
    seg = lax.axis_index("segment")
    d = lax.axis_index("dp")
    core = lax.rem(d, 2)
    xc = lax.rem(lax.div(d, 2), 4)
    zc = lax.div(d, 8)

    def dev(z, x, c):
        return {"dp": (z * 4 + x) * 2 + c}

    def put(src, dst, ssem, rsem, where):
        return pltpu.make_async_remote_copy(
            src_ref=src, dst_ref=dst, send_sem=ssem, recv_sem=rsem,
            device_id=where, device_id_type=pl.DeviceIdType.MESH)

    barrier = pltpu.get_barrier_semaphore()

    def greet(where):
        pl.semaphore_signal(barrier, inc=1, device_id=where, device_id_type=pl.DeviceIdType.MESH)

    greet({"segment": lax.rem(seg + 1, 4)})
    greet({"segment": lax.rem(seg + 3, 4)})
    greet(dev(zc, xc, 1 - core))
    for r in range(1, 4):
        for c in range(2):
            greet(dev(lax.rem(zc + r, 4), xc, c))
            greet(dev(zc, lax.rem(xc + r, 4), c))

    count = groups[0] * 4 - 3

    def keep(i):
        return jnp.where(i < count, 1.0, 0.0).astype(F32)

    zero_patch = jnp.zeros((K3, PIX), BF)
    sp[0:K3, :] = zero_patch
    sp[K3:2 * K3, :] = zero_patch
    sp[11 * K3:, :] = jnp.zeros((C, PIX), BF)
    dp_[9 * K3:10 * K3, :] = zero_patch
    dp_[10 * K3:11 * K3, :] = zero_patch
    gain_b[...] = jnp.broadcast_to(gain[...], (PIX, C)).T
    gain_acc[...] = jnp.zeros((C, PIX), F32)

    def transpose_weight():
        for tap in range(27):
            wt[:, (26 - tap) * C:(27 - tap) * C] = weight[:, tap * C:(tap + 1) * C].T

    @pl.when(seg == 0)
    def _():
        for i in range(F):
            xin[i] = (video[i].astype(F32) * keep(i)).astype(BF)

    @pl.when(seg == 3)
    def _():
        for i in range(F):
            dyin[i] = cot[i]

    @pl.when(seg >= 2)
    def _():
        transpose_weight()

    pl.semaphore_wait(barrier, 15)

    def fwd_copy(i):
        return put(feat.at[i], xin.at[i], fsend.at[i], frecv.at[i], {"segment": lax.rem(seg + 1, 4)})

    def bwd_copy(i):
        return put(dysend.at[i], dyin.at[i], bsend.at[i], brecv.at[i], {"segment": lax.rem(seg + 3, 4)})

    def forward(i, carry):
        @pl.when(seg > 0)
        def _():
            fwd_copy(i).wait_recv()

        x = xin[i].astype(F32)
        scale = lax.rsqrt(jnp.sum(x * x, axis=0, keepdims=True) * (1.0 / C) + EPS)
        scales[i] = scale
        normed = (x * scale * gain_b[...]).astype(BF)
        store_patches(sp, pl.multiple_of((i + 2) * K3, 64), normed)
        window = sp[pl.ds(pl.multiple_of(i * K3, 64), KK), :]
        conv = jnp.dot(weight[...], window, preferred_element_type=F32)
        sig = 1.0 / (1.0 + jnp.exp(-conv))
        feat[i] = ((x + conv * sig) * keep(i)).astype(BF)

        @pl.when(seg < 3)
        def _():
            fwd_copy(i).start()

        fac[i] = sig * (1.0 + conv * (1.0 - sig))
        return carry

    lax.fori_loop(0, F, forward, 0)

    @pl.when(seg < 2)
    def _():
        transpose_weight()

    def backward(n, carry):
        i = F - 1 - n

        @pl.when(seg < 3)
        def _():
            bwd_copy(i).wait_recv()

        dz = dyin[i].astype(F32) * keep(i)
        dconv = (dz * fac[i]).astype(BF)
        dconv_all[:, pl.ds(pl.multiple_of(i * PIX, PIX), PIX)] = dconv
        store_patches(dp_, pl.multiple_of(i * K3, 64), dconv)
        window = dp_[pl.ds(pl.multiple_of(i * K3, 64), KK), :]
        dnormed = jnp.dot(wt[...], window, preferred_element_type=F32)
        x = xin[i].astype(F32)
        scale = scales[i]
        gx = dnormed * gain_b[...]
        inner = jnp.sum(gx * x, axis=0, keepdims=True)
        dx = scale * gx - x * (scale * scale * scale * inner * (1.0 / C)) + dz
        dysend[i] = dx.astype(BF)

        @pl.when(seg > 0)
        def _():
            bwd_copy(i).start()

        gain_acc[...] += dnormed * x * scale
        return carry

    lax.fori_loop(0, F, backward, 0)

    row = lax.broadcasted_iota(jnp.int32, (C, C), 0)
    colm = lax.broadcasted_iota(jnp.int32, (C, C), 1)
    blk = lax.div(row, 12)
    source = (lax.rem(blk, 4) * 4 + lax.div(blk, 4)) * 12 + lax.rem(row, 12)
    perm = jnp.where(colm == source, 1.0, 0.0).astype(BF)
    dconv_perm[...] = jnp.dot(perm, dconv_all[...], preferred_element_type=F32).astype(BF)
    gain_perm = jnp.dot(perm, gain_acc[...].astype(BF), preferred_element_type=F32).astype(BF)

    def stage0(h, half):
        src, dst = ((a0, b0), (a1, b1))[h]
        return put(src.at[half], dst, s0send.at[h], s0recv.at[h], dev(zc, xc, 1 - core))

    def weight_part(lhs, dst, half, start, chunks):
        off = 0
        for size in chunks:
            col = pl.multiple_of(half * HALF + start + off, 128)
            rhs = jnp.concatenate([sp[pl.ds(f * K3 + col, size), :] for f in range(F)], axis=1)
            dst[half, :, off:off + size] = lax.dot_general(
                lhs[...], rhs, NT, preferred_element_type=F32).astype(BF)
            off += size

    def weight_half(n, carry):
        half = jnp.where(n == 0, 1 - core, core)
        weight_part(dconv_all, a0, half, 0, (768, 640))

        @pl.when(n == 0)
        def _():
            stage0(0, half).start()

        weight_part(dconv_perm, a1, half, N0, (640, 640))
        a1[half, :, N1 - 128:] = jnp.where(half == 1, gain_perm, a1[half, :, N1 - 128:])

        @pl.when(n == 0)
        def _():
            stage0(1, half).start()

        return carry

    lax.fori_loop(0, 2, weight_half, 0)

    def stage1(h, r):
        if h == 0:
            to = lax.rem(zc + r, 4)
            return put(c0.at[to], d0.at[r - 1], s1send.at[h, r - 1], s1recv.at[h, r - 1], dev(to, xc, core))
        to = lax.rem(xc + r, 4)
        return put(c1.at[to], d1.at[r - 1], s1send.at[h, r - 1], s1recv.at[h, r - 1], dev(zc, to, core))

    for h in range(2):
        stage0(h, 1 - core).wait_recv()
        mine, other, out = ((a0, b0, c0), (a1, b1, c1))[h]
        for q in range(4):
            rows = slice(q * 48, (q + 1) * 48)
            out[q] = (mine[core, rows, :].astype(F32) + other[rows, :].astype(F32)).astype(BF)
        for r in (2, 1, 3):
            stage1(h, r).start()

    prow = lax.broadcasted_iota(jnp.int32, (64, 48), 0)
    pcol = lax.broadcasted_iota(jnp.int32, (64, 48), 1)
    spread = jnp.where((lax.rem(prow, 8) < 6) & (pcol == lax.div(prow, 8) * 6 + lax.rem(prow, 8)), 1.0, 0.0).astype(BF)

    def stage2(h, r, c):
        if h == 0:
            to = lax.rem(xc + r, 4)
            where, src, dst = dev(zc, to, c), f0, g0
        else:
            to = lax.rem(zc + r, 4)
            where, src, dst = dev(to, xc, c), f1, g1
        slot = r * 2 + jnp.where(c == core, 0, 1)
        return put(src.at[to * 2 + c], dst.at[core * 4 + r], s2send.at[h, slot], s2recv.at[h, slot], where)

    for h in range(2):
        own, got, out = ((c0, d0, f0), (c1, d1, f1))[h]
        me = zc if h == 0 else xc
        for r in range(1, 4):
            stage1(h, r).wait_recv()
        total = own[me].astype(F32)
        for r in range(3):
            total = total + got[r].astype(F32)
        spaced = jnp.dot(spread, total.astype(BF), preferred_element_type=F32).astype(BF)
        for k in range(8):
            out[k] = spaced[k * 8:(k + 1) * 8, :]
        for r in (2, 1, 3):
            stage2(h, r, core).start()
            stage2(h, r, 1 - core).start()
        stage2(h, 0, 1 - core).start()

    def stage2_wait(h, r, c):
        slot = r * 2 + jnp.where(c == core, 0, 1)
        src, dst = ((f0, g0), (f1, g1))[h]
        where = dev(zc, lax.rem(xc + r, 4), c) if h == 0 else dev(lax.rem(zc + r, 4), xc, c)
        return put(src.at[0], dst.at[c * 4 + r], s2send.at[h, slot], s2recv.at[h, slot], where)

    for h in range(2):
        src, dst = ((f0, g0), (f1, g1))[h]
        mine = (xc if h == 0 else zc) * 2 + core
        dst[core * 4] = src[mine]
        for r in range(4):
            if r:
                stage2_wait(h, r, core).wait_recv()
            stage2_wait(h, r, 1 - core).wait_recv()
        for c in range(2):
            total = dst[c * 4].astype(F32)
            for r in range(1, 4):
                total = total + dst[c * 4 + r].astype(F32)
            start = c * HALF + (0 if h == 0 else N0)
            size = min(N0 if h == 0 else N1, KK - start)
            dweight[:, start:start + size] = total[0:6, 0:size]
            if h == 1 and c == 1:
                per_row = jnp.sum(total[:, N1 - 128:], axis=1, keepdims=True)
                r8 = lax.broadcasted_iota(jnp.int32, (8, 128), 0)
                l8 = lax.broadcasted_iota(jnp.int32, (8, 128), 1)
                line = jnp.sum(jnp.where(r8 == l8, per_row, 0.0), axis=0, keepdims=True)
                dgain[...] = line[:, 0:6]

    @pl.when(seg < 3)
    def _():
        def done(i, carry):
            fwd_copy(i).wait_send()
            return carry
        lax.fori_loop(0, F, done, 0)

    @pl.when(seg > 0)
    def _():
        def done(i, carry):
            bwd_copy(i).wait_send()
            return carry
        lax.fori_loop(0, F, done, 0)

    for h in range(2):
        stage0(h, 1 - core).wait_send()
        for r in range(1, 4):
            stage1(h, r).wait_send()
            stage2_wait(h, r, core).wait_send()
            stage2_wait(h, r, 1 - core).wait_send()
        stage2_wait(h, 0, 1 - core).wait_send()


def body(video_clips, conv_weight, norm_gain, cotangent, clip_groups):
    vmem = pl.BlockSpec(memory_space=pltpu.VMEM)
    smem = pl.BlockSpec(memory_space=pltpu.SMEM)
    dma = pltpu.SemaphoreType.DMA
    feat, dweight, dgain = pl.pallas_call(
        kernel,
        out_shape=(
            jax.ShapeDtypeStruct((F, C, PIX), BF),
            jax.ShapeDtypeStruct((6, KK), F32),
            jax.ShapeDtypeStruct((1, 6), F32),
        ),
        in_specs=[smem, vmem, vmem, vmem, vmem],
        out_specs=(vmem, vmem, vmem),
        scratch_shapes=[
            pltpu.VMEM((F, C, PIX), BF),
            pltpu.VMEM((F, C, PIX), BF),
            pltpu.VMEM((F, C, PIX), BF),
            pltpu.VMEM((F, C, PIX), F32),
            pltpu.VMEM((F, 1, PIX), F32),
            pltpu.VMEM((C, PIX), F32),
            pltpu.VMEM((C, PIX), F32),
            pltpu.VMEM((11 * K3 + C, PIX), BF),
            pltpu.VMEM((11 * K3, PIX), BF),
            pltpu.VMEM((C, KK), BF),
            pltpu.VMEM((C, F * PIX), BF),
            pltpu.VMEM((C, F * PIX), BF),
            pltpu.VMEM((2, C, N0), BF),
            pltpu.VMEM((2, C, N1), BF),
            pltpu.VMEM((C, N0), BF),
            pltpu.VMEM((C, N1), BF),
            pltpu.VMEM((4, 48, N0), BF),
            pltpu.VMEM((4, 48, N1), BF),
            pltpu.VMEM((3, 48, N0), BF),
            pltpu.VMEM((3, 48, N1), BF),
            pltpu.VMEM((8, 8, N0), BF),
            pltpu.VMEM((8, 8, N1), BF),
            pltpu.VMEM((8, 8, N0), BF),
            pltpu.VMEM((8, 8, N1), BF),
            dma((F,)), dma((F,)), dma((F,)), dma((F,)),
            dma((2,)), dma((2,)),
            dma((2, 3)), dma((2, 3)),
            dma((2, 8)), dma((2, 8)),
        ],
        compiler_params=pltpu.CompilerParams(
            collective_id=0, has_side_effects=True, vmem_limit_bytes=56 << 20),
    )(clip_groups, video_clips[0], conv_weight[0], norm_gain, cotangent[0])
    return (feat[None, None], dweight[None], dgain)


def solution(mesh):
    placed = (
        P("dp", None, None, None),
        P("segment", None, None),
        P("segment", None),
        P("dp", None, None, None),
        P("dp"),
    )
    return jax.shard_map(
        body,
        mesh=mesh,
        in_specs=placed,
        out_specs=(
            P("segment", "dp", None, None, None),
            P("segment", "dp", None),
            P("segment", "dp"),
        ),
        check_vma=False,
    )
```

```python
import jax
import jax.numpy as jnp
from jax import lax
from jax.experimental import pallas as pl
from jax.experimental.pallas import tpu as pltpu
from jax.sharding import PartitionSpec as P

TILE_H = 8
TILE_W = 16
EPS = 1e-06

F = 9
C = 192
PIX = 128
K3 = 9 * C
KK = 27 * C
N0 = 1408
N1 = 1280
HALF = N0 + N1

BF = jnp.bfloat16
F32 = jnp.float32
NT = (((1,), (1,)), ((), ()))


def tap_masks():
    lane = lax.broadcasted_iota(jnp.int32, (1, PIX), 1)
    col = lane & (TILE_W - 1)
    masks = []
    for a in range(3):
        for b in range(3):
            pos = lane + TILE_W * (a - 1)
            ok = (col + (b - 1) >= 0) & (col + (b - 1) < TILE_W) & (pos >= 0) & (pos < PIX)
            masks.append(jnp.where(ok, 1.0, 0.0).astype(BF))
    return masks


def store_patches(dst, base, frame):
    masks = tap_masks()
    values = []
    for a in range(3):
        for b in range(3):
            k = a * 3 + b
            shift = (-(TILE_W * (a - 1) + (b - 1))) % PIX
            values.append(frame if shift == 0 else pltpu.roll(frame, shift, 1) * masks[k])
    patches = jnp.concatenate(values, axis=0)
    dst[pl.ds(base, K3), :] = patches
    return patches


def kernel(groups, video, weight_hbm, gain, cot, feat_hbm, dweight_hbm, dgain_hbm,
           weight, feat, video_v, dweight, dgain, pre,
           xin, dyin, dysend, fac, scales, gain_b, gain_acc, sp, dp_, wt, dconv_all, dconv_perm,
           a0, a1, b0, b1, c0, c1, d0, d1, f0, f1, g0, g1,
           insem, outsem, featsem, fsend, frecv, bsend, brecv, s0send, s0recv, s1send, s1recv, s2send, s2recv):
    seg = lax.axis_index("segment")
    d = lax.axis_index("dp")
    core = lax.rem(d, 2)
    xc = lax.rem(lax.div(d, 2), 4)
    zc = lax.div(d, 8)

    def dev(z, x, c):
        return {"dp": (z * 4 + x) * 2 + c}

    def put(src, dst, ssem, rsem, where):
        return pltpu.make_async_remote_copy(
            src_ref=src, dst_ref=dst, send_sem=ssem, recv_sem=rsem,
            device_id=where, device_id_type=pl.DeviceIdType.MESH)

    early = pltpu.make_async_copy(weight_hbm.at[:, 2 * K3:], weight.at[:, 2 * K3:], insem.at[0])
    late = pltpu.make_async_copy(weight_hbm.at[:, :2 * K3], weight.at[:, :2 * K3], insem.at[1])
    clip = pltpu.make_async_copy(video, video_v, insem.at[2])
    target = pltpu.make_async_copy(cot, dyin, insem.at[2])

    @pl.when(seg == 0)
    def _():
        clip.start()

    early.start()
    late.start()

    @pl.when(seg == 3)
    def _():
        target.start()

    barrier = pltpu.get_barrier_semaphore()

    def greet(where):
        pl.semaphore_signal(barrier, inc=1, device_id=where, device_id_type=pl.DeviceIdType.MESH)

    greet({"segment": lax.rem(seg + 1, 4)})
    greet({"segment": lax.rem(seg + 3, 4)})
    greet(dev(zc, xc, 1 - core))
    for r in range(1, 4):
        for c in range(2):
            greet(dev(lax.rem(zc + r, 4), xc, c))
            greet(dev(zc, lax.rem(xc + r, 4), c))

    count = groups[0] * 4 - 3

    def keep(i):
        return jnp.where(i < count, 1.0, 0.0).astype(F32)

    zero_patch = jnp.zeros((K3, PIX), BF)
    sp[0:K3, :] = zero_patch
    sp[K3:2 * K3, :] = zero_patch
    sp[11 * K3:, :] = jnp.zeros((C, PIX), BF)
    dp_[0:K3, :] = zero_patch
    dp_[K3:2 * K3, :] = zero_patch
    pre[...] = jnp.zeros((C, PIX), F32)
    gain_b[...] = jnp.broadcast_to(gain[...], (PIX, C)).T
    gain_acc[...] = jnp.zeros((C, PIX), F32)

    def transpose_weight():
        for tap in range(27):
            to = (tap // 9) * 9 + 8 - tap % 9
            wt[:, to * C:(to + 1) * C] = weight[:, tap * C:(tap + 1) * C].T

    @pl.when(seg == 0)
    def _():
        clip.wait()
        for i in range(F):
            xin[i] = (video_v[i].astype(F32) * keep(i)).astype(BF)

    early.wait()
    late.wait()

    @pl.when(seg >= 2)
    def _():
        transpose_weight()


    def fwd_copy(i):
        return put(feat.at[i], xin.at[i], fsend.at[i], frecv.at[i], {"segment": lax.rem(seg + 1, 4)})

    def bwd_copy(i):
        return put(dysend.at[i], dyin.at[i], bsend.at[i], brecv.at[i], {"segment": lax.rem(seg + 3, 4)})

    def keep_copy(i):
        return pltpu.make_async_copy(feat.at[i], feat_hbm.at[i], featsem.at[i])

    def forward(i, carry):
        @pl.when(seg > 0)
        def _():
            fwd_copy(i).wait_recv()

        x = xin[i].astype(F32)
        scale = lax.rsqrt(jnp.sum(x * x, axis=0, keepdims=True) * (1.0 / C) + EPS)
        scales[i] = scale
        normed = (x * scale * gain_b[...]).astype(BF)
        patches = store_patches(sp, pl.multiple_of((i + 2) * K3, 64), normed)
        conv = pre[...] + jnp.dot(weight[:, 2 * K3:], patches, preferred_element_type=F32)
        sig = 1.0 / (1.0 + jnp.exp(-conv))
        feat[i] = ((x + conv * sig) * keep(i)).astype(BF)

        @pl.when(i == 0)
        def _():
            pl.semaphore_wait(barrier, 15)

        @pl.when(seg < 3)
        def _():
            fwd_copy(i).start()

        keep_copy(i).start()
        fac[i] = sig * (1.0 + conv * (1.0 - sig))
        window = sp[pl.ds(pl.multiple_of((i + 1) * K3, 64), 2 * K3), :]
        pre[...] = jnp.dot(weight[:, :2 * K3], window, preferred_element_type=F32)
        return carry

    lax.fori_loop(0, F, forward, 0)

    @pl.when(seg < 2)
    def _():
        transpose_weight()

    pre[...] = jnp.zeros((C, PIX), F32)

    @pl.when(seg == 3)
    def _():
        target.wait()

    def backward(n, carry):
        i = F - 1 - n

        @pl.when(seg < 3)
        def _():
            bwd_copy(i).wait_recv()

        dz = dyin[i].astype(F32) * keep(i)
        dconv = (dz * fac[i]).astype(BF)
        dconv_all[:, pl.ds(pl.multiple_of(i * PIX, PIX), PIX)] = dconv
        patches = store_patches(dp_, pl.multiple_of((n + 2) * K3, 64), dconv)
        dnormed = pre[...] + jnp.dot(wt[:, 2 * K3:], patches, preferred_element_type=F32)
        x = xin[i].astype(F32)
        scale = scales[i]
        gx = dnormed * gain_b[...]
        inner = jnp.sum(gx * x, axis=0, keepdims=True)
        dx = scale * gx - x * (scale * scale * scale * inner * (1.0 / C)) + dz
        dysend[i] = dx.astype(BF)

        @pl.when(seg > 0)
        def _():
            bwd_copy(i).start()

        gain_acc[...] += dnormed * x * scale
        window = dp_[pl.ds(pl.multiple_of((n + 1) * K3, 64), 2 * K3), :]
        pre[...] = jnp.dot(wt[:, :2 * K3], window, preferred_element_type=F32)
        return carry

    lax.fori_loop(0, F, backward, 0)

    row = lax.broadcasted_iota(jnp.int32, (C, C), 0)
    colm = lax.broadcasted_iota(jnp.int32, (C, C), 1)
    blk = lax.div(row, 12)
    source = (lax.rem(blk, 4) * 4 + lax.div(blk, 4)) * 12 + lax.rem(row, 12)
    perm = jnp.where(colm == source, 1.0, 0.0).astype(BF)
    dconv_perm[...] = jnp.dot(perm, dconv_all[...], preferred_element_type=F32).astype(BF)
    gain_perm = jnp.dot(perm, gain_acc[...].astype(BF), preferred_element_type=F32).astype(BF)

    def stage0(h, half):
        src, dst = ((a0, b0), (a1, b1))[h]
        return put(src.at[half], dst, s0send.at[h], s0recv.at[h], dev(zc, xc, 1 - core))

    def weight_part(lhs, dst, half, start, chunks):
        off = 0
        for size in chunks:
            col = pl.multiple_of(half * HALF + start + off, 128)
            rhs = jnp.concatenate([sp[pl.ds(f * K3 + col, size), :] for f in range(F)], axis=1)
            dst[half, :, off:off + size] = lax.dot_general(
                lhs[...], rhs, NT, preferred_element_type=F32).astype(BF)
            off += size

    def weight_half(n, carry):
        half = jnp.where(n == 0, 1 - core, core)
        weight_part(dconv_all, a0, half, 0, (768, 640))

        @pl.when(n == 0)
        def _():
            stage0(0, half).start()

        weight_part(dconv_perm, a1, half, N0, (640, 640))
        a1[half, :, N1 - 128:] = jnp.where(half == 1, gain_perm, a1[half, :, N1 - 128:])

        @pl.when(n == 0)
        def _():
            stage0(1, half).start()

        return carry

    lax.fori_loop(0, 2, weight_half, 0)

    def stage1(h, r):
        if h == 0:
            to = lax.rem(zc + r, 4)
            return put(c0.at[to], d0.at[r - 1], s1send.at[h, r - 1], s1recv.at[h, r - 1], dev(to, xc, core))
        to = lax.rem(xc + r, 4)
        return put(c1.at[to], d1.at[r - 1], s1send.at[h, r - 1], s1recv.at[h, r - 1], dev(zc, to, core))

    for h in range(2):
        stage0(h, 1 - core).wait_recv()
        mine, other, out = ((a0, b0, c0), (a1, b1, c1))[h]
        for q in range(4):
            rows = slice(q * 48, (q + 1) * 48)
            out[q] = (mine[core, rows, :].astype(F32) + other[rows, :].astype(F32)).astype(BF)
        for r in (2, 1, 3):
            stage1(h, r).start()

    prow = lax.broadcasted_iota(jnp.int32, (64, 48), 0)
    pcol = lax.broadcasted_iota(jnp.int32, (64, 48), 1)
    spread = jnp.where((lax.rem(prow, 8) < 6) & (pcol == lax.div(prow, 8) * 6 + lax.rem(prow, 8)), 1.0, 0.0).astype(BF)

    def stage2(h, r, c):
        if h == 0:
            to = lax.rem(xc + r, 4)
            where, src, dst = dev(zc, to, c), f0, g0
        else:
            to = lax.rem(zc + r, 4)
            where, src, dst = dev(to, xc, c), f1, g1
        slot = r * 2 + jnp.where(c == core, 0, 1)
        return put(src.at[to * 2 + c], dst.at[core * 4 + r], s2send.at[h, slot], s2recv.at[h, slot], where)

    for h in range(2):
        own, got, out = ((c0, d0, f0), (c1, d1, f1))[h]
        me = zc if h == 0 else xc
        for r in range(1, 4):
            stage1(h, r).wait_recv()
        total = own[me].astype(F32)
        for r in range(3):
            total = total + got[r].astype(F32)
        spaced = jnp.dot(spread, total.astype(BF), preferred_element_type=F32).astype(BF)
        for k in range(8):
            out[k] = spaced[k * 8:(k + 1) * 8, :]
        for r in (2, 1, 3):
            stage2(h, r, core).start()
            stage2(h, r, 1 - core).start()
        stage2(h, 0, 1 - core).start()

    def stage2_wait(h, r, c):
        slot = r * 2 + jnp.where(c == core, 0, 1)
        src, dst = ((f0, g0), (f1, g1))[h]
        where = dev(zc, lax.rem(xc + r, 4), c) if h == 0 else dev(lax.rem(zc + r, 4), xc, c)
        return put(src.at[0], dst.at[c * 4 + r], s2send.at[h, slot], s2recv.at[h, slot], where)

    for h in range(2):
        src, dst = ((f0, g0), (f1, g1))[h]
        mine = (xc if h == 0 else zc) * 2 + core
        dst[core * 4] = src[mine]
        for r in range(4):
            if r:
                stage2_wait(h, r, core).wait_recv()
            stage2_wait(h, r, 1 - core).wait_recv()
        for c in range(2):
            total = dst[c * 4].astype(F32)
            for r in range(1, 4):
                total = total + dst[c * 4 + r].astype(F32)
            start = c * HALF + (0 if h == 0 else N0)
            size = min(N0 if h == 0 else N1, KK - start)
            for j in range(6):
                dweight[j, :, start:start + size] = total[j:j + 1, 0:size]
            if h == 1 and c == 1:
                per_row = jnp.sum(total[:, N1 - 128:], axis=1, keepdims=True)
                r8 = lax.broadcasted_iota(jnp.int32, (8, 128), 0)
                l8 = lax.broadcasted_iota(jnp.int32, (8, 128), 1)
                line = jnp.sum(jnp.where(r8 == l8, per_row, 0.0), axis=0, keepdims=True)
                dgain[...] = line

    results = (pltpu.make_async_copy(dweight, dweight_hbm, outsem.at[0]),
               pltpu.make_async_copy(dgain, dgain_hbm, outsem.at[1]))
    for result in results:
        result.start()

    def kept(i, carry):
        keep_copy(i).wait()
        return carry

    lax.fori_loop(0, F, kept, 0)

    @pl.when(seg < 3)
    def _():
        def done(i, carry):
            fwd_copy(i).wait_send()
            return carry
        lax.fori_loop(0, F, done, 0)

    @pl.when(seg > 0)
    def _():
        def done(i, carry):
            bwd_copy(i).wait_send()
            return carry
        lax.fori_loop(0, F, done, 0)

    for h in range(2):
        stage0(h, 1 - core).wait_send()
        for r in range(1, 4):
            stage1(h, r).wait_send()
            stage2_wait(h, r, core).wait_send()
            stage2_wait(h, r, 1 - core).wait_send()
        stage2_wait(h, 0, 1 - core).wait_send()
    for result in results:
        result.wait()


def hand_over(feat, dweight, dgain, feat_out, dweight_out, dgain_out):
    feat_out[...] = feat[...]
    dweight_out[...] = dweight[...]
    dgain_out[...] = dgain[:, 0:6]


def body(video_clips, conv_weight, norm_gain, cotangent, clip_groups):
    vmem = pl.BlockSpec(memory_space=pltpu.VMEM)
    hbm = pl.BlockSpec(memory_space=pl.ANY)
    smem = pl.BlockSpec(memory_space=pltpu.SMEM)
    dma = pltpu.SemaphoreType.DMA
    feat, dweight, dgain = pl.pallas_call(
        kernel,
        out_shape=(
            jax.ShapeDtypeStruct((F, C, PIX), BF),
            jax.ShapeDtypeStruct((6, 1, KK), F32),
            jax.ShapeDtypeStruct((1, 128), F32),
        ),
        in_specs=[smem, hbm, hbm, vmem, hbm],
        out_specs=(hbm, hbm, hbm),
        scratch_shapes=[
            pltpu.VMEM((C, KK), BF),
            pltpu.VMEM((F, C, PIX), BF),
            pltpu.VMEM((F, C, PIX), BF),
            pltpu.VMEM((6, 1, KK), F32),
            pltpu.VMEM((1, 128), F32),
            pltpu.VMEM((C, PIX), F32),
            pltpu.VMEM((F, C, PIX), BF),
            pltpu.VMEM((F, C, PIX), BF),
            pltpu.VMEM((F, C, PIX), BF),
            pltpu.VMEM((F, C, PIX), F32),
            pltpu.VMEM((F, 1, PIX), F32),
            pltpu.VMEM((C, PIX), F32),
            pltpu.VMEM((C, PIX), F32),
            pltpu.VMEM((11 * K3 + C, PIX), BF),
            pltpu.VMEM((11 * K3, PIX), BF),
            pltpu.VMEM((C, KK), BF),
            pltpu.VMEM((C, F * PIX), BF),
            pltpu.VMEM((C, F * PIX), BF),
            pltpu.VMEM((2, C, N0), BF),
            pltpu.VMEM((2, C, N1), BF),
            pltpu.VMEM((C, N0), BF),
            pltpu.VMEM((C, N1), BF),
            pltpu.VMEM((4, 48, N0), BF),
            pltpu.VMEM((4, 48, N1), BF),
            pltpu.VMEM((3, 48, N0), BF),
            pltpu.VMEM((3, 48, N1), BF),
            pltpu.VMEM((8, 8, N0), BF),
            pltpu.VMEM((8, 8, N1), BF),
            pltpu.VMEM((8, 8, N0), BF),
            pltpu.VMEM((8, 8, N1), BF),
            dma((3,)), dma((2,)), dma((F,)),
            dma((F,)), dma((F,)), dma((F,)), dma((F,)),
            dma((2,)), dma((2,)),
            dma((2, 3)), dma((2, 3)),
            dma((2, 8)), dma((2, 8)),
        ],
        compiler_params=pltpu.CompilerParams(
            collective_id=0, has_side_effects=True, vmem_limit_bytes=56 << 20),
    )(clip_groups, video_clips[0], conv_weight[0], norm_gain, cotangent[0])
    feat, dweight, dgain = pl.pallas_call(
        hand_over,
        out_shape=(
            jax.ShapeDtypeStruct((F, C, PIX), BF),
            jax.ShapeDtypeStruct((6, 1, KK), F32),
            jax.ShapeDtypeStruct((1, 6), F32),
        ),
        in_specs=[vmem, vmem, vmem],
        out_specs=(vmem, vmem, vmem),
    )(feat, dweight, dgain)
    return (feat[None, None], jnp.transpose(dweight, (1, 0, 2)), dgain)


def solution(mesh):
    placed = (
        P("dp", None, None, None),
        P("segment", None, None),
        P("segment", None),
        P("dp", None, None, None),
        P("dp"),
    )
    return jax.shard_map(
        body,
        mesh=mesh,
        in_specs=placed,
        out_specs=(
            P("segment", "dp", None, None, None),
            P("segment", "dp", None),
            P("segment", "dp"),
        ),
        check_vma=False,
    )
```

```python
import jax
import jax.numpy as jnp
from jax import lax
from jax.experimental import pallas as pl
from jax.experimental.pallas import tpu as pltpu
from jax.sharding import PartitionSpec as P

TILE_H = 8
TILE_W = 16
EPS = 1e-06

F = 9
C = 192
PIX = 128
K3 = 9 * C
KK = 27 * C
HK = K3 // 2
N0 = 512
N1 = 384

BF = jnp.bfloat16
F32 = jnp.float32
NT = (((1,), (1,)), ((), ()))


def tap_masks():
    lane = lax.broadcasted_iota(jnp.int32, (1, PIX), 1)
    col = lane & (TILE_W - 1)
    masks = []
    for a in range(3):
        for b in range(3):
            pos = lane + TILE_W * (a - 1)
            ok = (col + (b - 1) >= 0) & (col + (b - 1) < TILE_W) & (pos >= 0) & (pos < PIX)
            masks.append(jnp.where(ok, 1.0, 0.0).astype(BF))
    return masks


def store_patches(dst, base, frame):
    masks = tap_masks()
    values = []
    for a in range(3):
        for b in range(3):
            k = a * 3 + b
            shift = (-(TILE_W * (a - 1) + (b - 1))) % PIX
            values.append(frame if shift == 0 else pltpu.roll(frame, shift, 1) * masks[k])
    patches = jnp.concatenate(values, axis=0)
    dst[pl.ds(base, K3), :] = patches
    return patches


def kernel(groups, video, weight_hbm, gain, cot, feat_hbm, dweight_hbm, dgain_hbm,
           weight, feat, video_v, dweight, dgain, pre, xin, dyin, dysend, fac, scales, gain_b, gain_acc,
           sp, xsp, dp_, wt, dc, odc, acc0, acc1,
           c0, c1, cg, d0, d1, dg, fa0, fa1, fb0, fb1, fg, ga0, ga1, gb0, gb1, gg,
           insem, outsem, featsem, fsend, frecv, bsend, brecv, psend, precv, csend, crecv,
           s1send, s1recv, s2send, s2recv):
    seg = lax.axis_index("segment")
    d = lax.axis_index("dp")
    core = lax.rem(d, 2)
    xc = lax.rem(lax.div(d, 2), 4)
    zc = lax.div(d, 8)

    def dev(z, x, c):
        return {"dp": (z * 4 + x) * 2 + c}

    def put(src, dst, ssem, rsem, where):
        return pltpu.make_async_remote_copy(
            src_ref=src, dst_ref=dst, send_sem=ssem, recv_sem=rsem,
            device_id=where, device_id_type=pl.DeviceIdType.MESH)

    early = pltpu.make_async_copy(weight_hbm.at[:, 2 * K3:], weight.at[:, 2 * K3:], insem.at[0])
    late = pltpu.make_async_copy(weight_hbm.at[:, :2 * K3], weight.at[:, :2 * K3], insem.at[1])
    clip = pltpu.make_async_copy(video, video_v, insem.at[2])
    target = pltpu.make_async_copy(cot, dyin, insem.at[2])

    @pl.when(seg == 0)
    def _():
        clip.start()

    early.start()
    late.start()

    @pl.when(seg == 3)
    def _():
        target.start()

    barrier = pltpu.get_barrier_semaphore()

    def greet(where):
        pl.semaphore_signal(barrier, inc=1, device_id=where, device_id_type=pl.DeviceIdType.MESH)

    greet({"segment": lax.rem(seg + 1, 4)})
    greet({"segment": lax.rem(seg + 3, 4)})
    greet(dev(zc, xc, 1 - core))
    for r in range(1, 4):
        for c in range(2):
            greet(dev(lax.rem(zc + r, 4), xc, c))
            greet(dev(zc, lax.rem(xc + r, 4), c))

    count = groups[0] * 4 - 3

    def keep(i):
        return jnp.where(i < count, 1.0, 0.0).astype(F32)

    zero_patch = jnp.zeros((K3, PIX), BF)
    sp[0:K3, :] = zero_patch
    sp[K3:2 * K3, :] = zero_patch
    sp[11 * K3:, :] = jnp.zeros((32, PIX), BF)
    xsp[0:K3, :] = zero_patch
    xsp[11 * HK:, :] = jnp.zeros((32, PIX), BF)
    dp_[0:K3, :] = zero_patch
    dp_[K3:2 * K3, :] = zero_patch
    pre[...] = jnp.zeros((C, PIX), F32)
    gain_b[...] = jnp.broadcast_to(gain[...], (PIX, C)).T
    gain_acc[...] = jnp.zeros((C, PIX), F32)

    def transpose_weight():
        for tap in range(27):
            to = (tap // 9) * 9 + 8 - tap % 9
            wt[:, to * C:(to + 1) * C] = weight[:, tap * C:(tap + 1) * C].T

    @pl.when(seg == 0)
    def _():
        clip.wait()
        for i in range(F):
            xin[i] = (video_v[i].astype(F32) * keep(i)).astype(BF)

    early.wait()
    late.wait()

    @pl.when(seg >= 2)
    def _():
        transpose_weight()

    def fwd_copy(i):
        return put(feat.at[i], xin.at[i], fsend.at[i], frecv.at[i], {"segment": lax.rem(seg + 1, 4)})

    def bwd_copy(i):
        return put(dysend.at[i], dyin.at[i], bsend.at[i], brecv.at[i], {"segment": lax.rem(seg + 3, 4)})

    def keep_copy(i):
        return pltpu.make_async_copy(feat.at[i], feat_hbm.at[i], featsem.at[i])

    def pair_copy(i):
        src = pl.multiple_of((i + 2) * K3 + HK * (1 - core), 32)
        dst = pl.multiple_of((i + 2) * HK, 32)
        return put(sp.at[pl.ds(src, HK), :], xsp.at[pl.ds(dst, HK), :], psend.at[i], precv.at[i], dev(zc, xc, 1 - core))

    def dconv_copy(i):
        return put(dc.at[i], odc.at[i], csend.at[i], crecv.at[i], dev(zc, xc, 1 - core))

    def forward(i, carry):
        @pl.when(seg > 0)
        def _():
            fwd_copy(i).wait_recv()

        x = xin[i].astype(F32)
        scale = lax.rsqrt(jnp.sum(x * x, axis=0, keepdims=True) * (1.0 / C) + EPS)
        scales[i] = scale
        normed = (x * scale * gain_b[...]).astype(BF)
        patches = store_patches(sp, pl.multiple_of((i + 2) * K3, 64), normed)
        conv = pre[...] + jnp.dot(weight[:, 2 * K3:], patches, preferred_element_type=F32)
        sig = 1.0 / (1.0 + jnp.exp(-conv))
        feat[i] = ((x + conv * sig) * keep(i)).astype(BF)

        @pl.when(i == 0)
        def _():
            pl.semaphore_wait(barrier, 15)

        @pl.when(seg < 3)
        def _():
            fwd_copy(i).start()

        keep_copy(i).start()
        pair_copy(i).start()
        fac[i] = sig * (1.0 + conv * (1.0 - sig))
        window = sp[pl.ds(pl.multiple_of((i + 1) * K3, 64), 2 * K3), :]
        pre[...] = jnp.dot(weight[:, :2 * K3], window, preferred_element_type=F32)
        return carry

    lax.fori_loop(0, F, forward, 0)

    @pl.when(seg < 2)
    def _():
        transpose_weight()

    row = lax.broadcasted_iota(jnp.int32, (C, C), 0)
    colm = lax.broadcasted_iota(jnp.int32, (C, C), 1)
    blk = lax.div(row, 12)
    source = (lax.rem(blk, 4) * 4 + lax.div(blk, 4)) * 12 + lax.rem(row, 12)
    perm = jnp.where(colm == source, 1.0, 0.0).astype(BF)

    def stage1(t, h, r):
        to = lax.rem((zc if h == 0 else xc) + r, 4)
        where = dev(to, xc, core) if h == 0 else dev(zc, to, core)
        src, dst = ((c0, d0), (c1, d1))[h]
        return put(src.at[t, to], dst.at[t, r - 1], s1send.at[t * 2 + h, r - 1], s1recv.at[t * 2 + h, r - 1], where)

    def stage1_gain(r):
        to = lax.rem(zc + r, 4)
        return put(cg.at[to], dg.at[r - 1], s1send.at[6, r - 1], s1recv.at[6, r - 1], dev(to, xc, core))

    def emit(t, part0, part1):
        low = part0.astype(BF)
        high = jnp.dot(perm, part1.astype(BF), preferred_element_type=F32).astype(BF)
        for q in range(4):
            c0[t, q] = low[q * 48:(q + 1) * 48, :]
            c1[t, q] = high[q * 48:(q + 1) * 48, :]
        for r in (2, 1, 3):
            stage1(t, 0, r).start()
            stage1(t, 1, r).start()

    def emit_gain():
        low = gain_acc[...].astype(BF)
        for q in range(4):
            cg[q] = low[q * 48:(q + 1) * 48, :]
        for r in (2, 1, 3):
            stage1_gain(r).start()

    def patch_rows(t, i, start, size):
        own = pl.multiple_of((i + t) * K3 + HK * core + start, 32)
        other = pl.multiple_of((i + t) * HK + start, 32)
        return [sp[pl.ds(own, size), :], xsp[pl.ds(other, size), :]]

    def weight_product(t, frames, start, size):
        lhs, rhs = [], []
        for i in frames:
            lhs += [dc[i], odc[i]]
            rhs += patch_rows(t, i, start, size)
        return lax.dot_general(jnp.concatenate(lhs, axis=1), jnp.concatenate(rhs, axis=1), NT,
                               preferred_element_type=F32)

    pre[...] = jnp.zeros((C, PIX), F32)

    def wait_pairs():
        def body_(i, carry):
            pair_copy(i).wait_recv()
            return carry
        lax.fori_loop(0, F, body_, 0)

    @pl.when(seg == 3)
    def _():
        target.wait()

    def backward(n, carry):
        i = F - 1 - n

        @pl.when(seg < 3)
        def _():
            bwd_copy(i).wait_recv()

        dz = dyin[i].astype(F32) * keep(i)
        dconv = (dz * fac[i]).astype(BF)
        dc[i] = dconv
        patches = store_patches(dp_, pl.multiple_of((n + 2) * K3, 64), dconv)
        dnormed = pre[...] + jnp.dot(wt[:, 2 * K3:], patches, preferred_element_type=F32)
        x = xin[i].astype(F32)
        scale = scales[i]
        gx = dnormed * gain_b[...]
        inner = jnp.sum(gx * x, axis=0, keepdims=True)
        dx = scale * gx - x * (scale * scale * scale * inner * (1.0 / C)) + dz
        dysend[i] = dx.astype(BF)
        bwd_copy(i).start()
        dconv_copy(i).start()
        gain_acc[...] += dnormed * x * scale
        window = dp_[pl.ds(pl.multiple_of((n + 1) * K3, 64), 2 * K3), :]
        pre[...] = jnp.dot(wt[:, :2 * K3], window, preferred_element_type=F32)
        return carry

    @pl.when(seg > 0)
    def _():
        lax.fori_loop(0, F, backward, 0)
        emit_gain()
        wait_pairs()

        def arrived(i, carry):
            dconv_copy(i).wait_recv()
            return carry

        lax.fori_loop(0, F, arrived, 0)
        for t in range(3):
            frames = range(2 - t, F)
            emit(t, weight_product(t, frames, 0, N0), weight_product(t, frames, N0, N1))

    def take(n):
        i = F - 1 - n
        bwd_copy(i).wait_recv()
        dconv = (dyin[i].astype(F32) * keep(i) * fac[i]).astype(BF)
        dc[i] = dconv
        dconv_copy(i).start()
        store_patches(dp_, pl.multiple_of((n + 2) * K3, 64), dconv)

    def accumulate(t, i):
        acc0[t] += weight_product(t, [i], 0, N0)
        acc1[t] += weight_product(t, [i], N0, N1)

    @pl.when(seg == 0)
    def _():
        wait_pairs()
        acc0[...] = jnp.zeros((3, C, N0), F32)
        acc1[...] = jnp.zeros((3, C, N1), F32)
        take(0)

        def step(n, carry):
            take(n)
            i = F - n
            dconv_copy(i).wait_recv()
            for t in range(3):
                accumulate(t, i)
            return carry

        lax.fori_loop(1, F - 1, step, 0)
        emit(0, acc0[0], acc1[0])
        take(F - 1)
        dconv_copy(1).wait_recv()
        accumulate(1, 1)
        emit(1, acc0[1], acc1[1])
        accumulate(2, 1)
        dconv_copy(0).wait_recv()
        accumulate(2, 0)
        emit(2, acc0[2], acc1[2])

        def add_gain(n, dnormed):
            i = F - 1 - n
            gain_acc[...] += dnormed * xin[i].astype(F32) * scales[i]

        def two(j, carry):
            n = j * 2
            first = dp_[pl.ds(pl.multiple_of(n * K3, 64), KK), :]
            second = dp_[pl.ds(pl.multiple_of((n + 1) * K3, 64), KK), :]
            both = jnp.dot(wt[...], jnp.concatenate([first, second], axis=1), preferred_element_type=F32)
            add_gain(n, both[:, :PIX])
            add_gain(n + 1, both[:, PIX:])
            return carry

        lax.fori_loop(0, 4, two, 0)
        add_gain(8, jnp.dot(wt[...], dp_[8 * K3:8 * K3 + KK, :], preferred_element_type=F32))
        emit_gain()

    prow = lax.broadcasted_iota(jnp.int32, (64, 48), 0)
    pcol = lax.broadcasted_iota(jnp.int32, (64, 48), 1)
    spread = jnp.where((lax.rem(prow, 8) < 6) & (pcol == lax.div(prow, 8) * 6 + lax.rem(prow, 8)), 1.0, 0.0).astype(BF)

    batches = ((0, 0, fa0, ga0), (1, 1, fa1, ga1), (2, 0, fb0, gb0), (3, 1, fb1, gb1), (4, 0, fg, gg))

    def stage2(batch, r, c):
        k, h, src, dst = batch
        if h == 0:
            to = lax.rem(xc + r, 4)
            where = dev(zc, to, c)
        else:
            to = lax.rem(zc + r, 4)
            where = dev(to, xc, c)
        slot = r * 2 + jnp.where(c == core, 0, 1)
        return put(src.at[to * 2 + c], dst.at[core * 4 + r], s2send.at[k, slot], s2recv.at[k, slot], where)

    def send_batch(batch):
        for r in (2, 1, 3):
            stage2(batch, r, core).start()
            stage2(batch, r, 1 - core).start()
        stage2(batch, 0, 1 - core).start()

    def collect(own, got, out, part):
        total = own.astype(F32)
        for r in range(3):
            total = total + got[r].astype(F32)
        spaced = jnp.dot(spread, total.astype(BF), preferred_element_type=F32).astype(BF)
        for k in range(8):
            out[k, part] = spaced[k * 8:(k + 1) * 8, :]

    def finish_stage1(t, h):
        for r in range(1, 4):
            stage1(t, h, r).wait_recv()
        own, got = ((c0, d0), (c1, d1))[h]
        out = ((fa0, fa1), (fa0, fa1), (fb0, fb1))[t][h]
        collect(own[t, zc if h == 0 else xc], got[t], out, t % 2)

    for h in range(2):
        finish_stage1(0, h)
        finish_stage1(1, h)
        send_batch(batches[h])
    for h in range(2):
        finish_stage1(2, h)
        send_batch(batches[2 + h])
    for r in range(1, 4):
        stage1_gain(r).wait_recv()
    collect(cg[zc], dg[...], fg, 0)
    send_batch(batches[4])

    def stage2_wait(batch, r, c):
        k, h, src, dst = batch
        slot = r * 2 + jnp.where(c == core, 0, 1)
        where = dev(zc, lax.rem(xc + r, 4), c) if h == 0 else dev(lax.rem(zc + r, 4), xc, c)
        return put(src.at[0], dst.at[c * 4 + r], s2send.at[k, slot], s2recv.at[k, slot], where)

    for batch in batches:
        k, h, src, dst = batch
        mine = (xc if h == 0 else zc) * 2 + core
        dst[core * 4] = src[mine]
        for r in range(4):
            if r:
                stage2_wait(batch, r, core).wait_recv()
            stage2_wait(batch, r, 1 - core).wait_recv()
        if k == 4:
            total = dst[0, 0].astype(F32)
            for q in range(1, 8):
                total = total + dst[q, 0].astype(F32)
            per_row = jnp.sum(total, axis=1, keepdims=True)
            r8 = lax.broadcasted_iota(jnp.int32, (8, 128), 0)
            l8 = lax.broadcasted_iota(jnp.int32, (8, 128), 1)
            dgain[...] = jnp.sum(jnp.where(r8 == l8, per_row, 0.0), axis=0, keepdims=True)
            continue
        for part in range(2 if k < 2 else 1):
            t = part if k < 2 else 2
            for c in range(2):
                total = dst[c * 4, part].astype(F32)
                for r in range(1, 4):
                    total = total + dst[c * 4 + r, part].astype(F32)
                start = t * K3 + c * HK + (0 if h == 0 else N0)
                size = N0 if h == 0 else HK - N0
                for j in range(6):
                    dweight[j, :, start:start + size] = total[j:j + 1, 0:size]

    results = (pltpu.make_async_copy(dweight, dweight_hbm, outsem.at[0]),
               pltpu.make_async_copy(dgain, dgain_hbm, outsem.at[1]))
    for result in results:
        result.start()

    def settle(i, carry):
        keep_copy(i).wait()
        pair_copy(i).wait_send()
        dconv_copy(i).wait_send()

        @pl.when(seg < 3)
        def _():
            fwd_copy(i).wait_send()

        @pl.when(seg > 0)
        def _():
            bwd_copy(i).wait_send()

        return carry

    lax.fori_loop(0, F, settle, 0)
    for r in range(1, 4):
        for t in range(3):
            stage1(t, 0, r).wait_send()
            stage1(t, 1, r).wait_send()
        stage1_gain(r).wait_send()
    for batch in batches:
        for r in range(4):
            if r:
                stage2_wait(batch, r, core).wait_send()
            stage2_wait(batch, r, 1 - core).wait_send()
    for result in results:
        result.wait()


def hand_over(feat, dweight, dgain, feat_out, dweight_out, dgain_out):
    feat_out[...] = feat[...]
    dweight_out[...] = dweight[...]
    dgain_out[...] = dgain[:, 0:6]


def body(video_clips, conv_weight, norm_gain, cotangent, clip_groups):
    vmem = pl.BlockSpec(memory_space=pltpu.VMEM)
    hbm = pl.BlockSpec(memory_space=pl.ANY)
    smem = pl.BlockSpec(memory_space=pltpu.SMEM)
    dma = pltpu.SemaphoreType.DMA
    feat, dweight, dgain = pl.pallas_call(
        kernel,
        out_shape=(
            jax.ShapeDtypeStruct((F, C, PIX), BF),
            jax.ShapeDtypeStruct((6, 1, KK), F32),
            jax.ShapeDtypeStruct((1, 128), F32),
        ),
        in_specs=[smem, hbm, hbm, vmem, hbm],
        out_specs=(hbm, hbm, hbm),
        scratch_shapes=[
            pltpu.VMEM((C, KK), BF),
            pltpu.VMEM((F, C, PIX), BF),
            pltpu.VMEM((F, C, PIX), BF),
            pltpu.VMEM((6, 1, KK), F32),
            pltpu.VMEM((1, 128), F32),
            pltpu.VMEM((C, PIX), F32),
            pltpu.VMEM((F, C, PIX), BF),
            pltpu.VMEM((F, C, PIX), BF),
            pltpu.VMEM((F, C, PIX), BF),
            pltpu.VMEM((F, C, PIX), F32),
            pltpu.VMEM((F, 1, PIX), F32),
            pltpu.VMEM((C, PIX), F32),
            pltpu.VMEM((C, PIX), F32),
            pltpu.VMEM((11 * K3 + 32, PIX), BF),
            pltpu.VMEM((11 * HK + 32, PIX), BF),
            pltpu.VMEM((11 * K3, PIX), BF),
            pltpu.VMEM((C, KK), BF),
            pltpu.VMEM((F, C, PIX), BF),
            pltpu.VMEM((F, C, PIX), BF),
            pltpu.VMEM((3, C, N0), F32),
            pltpu.VMEM((3, C, N1), F32),
            pltpu.VMEM((3, 4, 48, N0), BF),
            pltpu.VMEM((3, 4, 48, N1), BF),
            pltpu.VMEM((4, 48, PIX), BF),
            pltpu.VMEM((3, 3, 48, N0), BF),
            pltpu.VMEM((3, 3, 48, N1), BF),
            pltpu.VMEM((3, 48, PIX), BF),
            pltpu.VMEM((8, 2, 8, N0), BF),
            pltpu.VMEM((8, 2, 8, N1), BF),
            pltpu.VMEM((8, 1, 8, N0), BF),
            pltpu.VMEM((8, 1, 8, N1), BF),
            pltpu.VMEM((8, 1, 8, PIX), BF),
            pltpu.VMEM((8, 2, 8, N0), BF),
            pltpu.VMEM((8, 2, 8, N1), BF),
            pltpu.VMEM((8, 1, 8, N0), BF),
            pltpu.VMEM((8, 1, 8, N1), BF),
            pltpu.VMEM((8, 1, 8, PIX), BF),
            dma((3,)), dma((2,)), dma((F,)),
            dma((F,)), dma((F,)), dma((F,)), dma((F,)),
            dma((F,)), dma((F,)), dma((F,)), dma((F,)),
            dma((7, 3)), dma((7, 3)),
            dma((5, 8)), dma((5, 8)),
        ],
        compiler_params=pltpu.CompilerParams(
            collective_id=0, has_side_effects=True, vmem_limit_bytes=56 << 20),
    )(clip_groups, video_clips[0], conv_weight[0], norm_gain, cotangent[0])
    feat, dweight, dgain = pl.pallas_call(
        hand_over,
        out_shape=(
            jax.ShapeDtypeStruct((F, C, PIX), BF),
            jax.ShapeDtypeStruct((6, 1, KK), F32),
            jax.ShapeDtypeStruct((1, 6), F32),
        ),
        in_specs=[vmem, vmem, vmem],
        out_specs=(vmem, vmem, vmem),
    )(feat, dweight, dgain)
    return (feat[None, None], jnp.transpose(dweight, (1, 0, 2)), dgain)


def solution(mesh):
    placed = (
        P("dp", None, None, None),
        P("segment", None, None),
        P("segment", None),
        P("dp", None, None, None),
        P("dp"),
    )
    return jax.shard_map(
        body,
        mesh=mesh,
        in_specs=placed,
        out_specs=(
            P("segment", "dp", None, None, None),
            P("segment", "dp", None),
            P("segment", "dp"),
        ),
        check_vma=False,
    )
```

```python
import jax
import jax.numpy as jnp
from jax import lax
from jax.experimental import pallas as pl
from jax.experimental.pallas import tpu as pltpu
from jax.sharding import PartitionSpec as P

TILE_H = 8
TILE_W = 16
EPS = 1e-06

F = 9
C = 192
PIX = 128
K3 = 9 * C
KK = 27 * C
HK = K3 // 2
N0 = 512
N1 = 384

BF = jnp.bfloat16
F32 = jnp.float32
NT = (((1,), (1,)), ((), ()))


def tap_masks():
    lane = lax.broadcasted_iota(jnp.int32, (1, PIX), 1)
    col = lane & (TILE_W - 1)
    masks = []
    for a in range(3):
        for b in range(3):
            pos = lane + TILE_W * (a - 1)
            ok = (col + (b - 1) >= 0) & (col + (b - 1) < TILE_W) & (pos >= 0) & (pos < PIX)
            masks.append(jnp.where(ok, 1.0, 0.0).astype(BF))
    return masks


def store_patches(dst, base, frame):
    masks = tap_masks()
    values = []
    for a in range(3):
        for b in range(3):
            k = a * 3 + b
            shift = (-(TILE_W * (a - 1) + (b - 1))) % PIX
            values.append(frame if shift == 0 else pltpu.roll(frame, shift, 1) * masks[k])
    patches = jnp.concatenate(values, axis=0)
    dst[pl.ds(base, K3), :] = patches
    return patches


def kernel(groups, video, weight_hbm, gain, cot, feat_hbm, dweight_hbm, dgain_hbm,
           weight, feat, video_v, dweight, dgain, pre, xin, dyin, dysend, fac, scales, gain_b, gain_acc,
           sp, xsp, dp_, wt, whalf, fold, dc, odc, acc0, acc1, col_sum,
           c0, c1, cg, d0, d1, dg, f0, f1, g0, g1,
           insem, outsem, featsem, fsend, frecv, bsend, brecv, psend, precv, csend, crecv,
           s1send, s1recv, s2send, s2recv):
    seg = lax.axis_index("segment")
    d = lax.axis_index("dp")
    core = lax.rem(d, 2)
    xc = lax.rem(lax.div(d, 2), 4)
    zc = lax.div(d, 8)

    def dev(z, x, c):
        return {"dp": (z * 4 + x) * 2 + c}

    def put(src, dst, ssem, rsem, where):
        return pltpu.make_async_remote_copy(
            src_ref=src, dst_ref=dst, send_sem=ssem, recv_sem=rsem,
            device_id=where, device_id_type=pl.DeviceIdType.MESH)

    early = pltpu.make_async_copy(weight_hbm.at[:, 2 * K3:], weight.at[:, 2 * K3:], insem.at[0])
    late = pltpu.make_async_copy(weight_hbm.at[:, :2 * K3], weight.at[:, :2 * K3], insem.at[1])
    clip = pltpu.make_async_copy(video, video_v, insem.at[2])
    target = pltpu.make_async_copy(cot, dyin, insem.at[2])

    @pl.when(seg == 0)
    def _():
        clip.start()

    early.start()
    late.start()

    @pl.when(seg == 3)
    def _():
        target.start()

    barrier = pltpu.get_barrier_semaphore()

    def greet(where):
        pl.semaphore_signal(barrier, inc=1, device_id=where, device_id_type=pl.DeviceIdType.MESH)

    greet({"segment": lax.rem(seg + 1, 4)})
    greet({"segment": lax.rem(seg + 3, 4)})
    greet(dev(zc, xc, 1 - core))
    for r in range(1, 4):
        for c in range(2):
            greet(dev(lax.rem(zc + r, 4), xc, c))
            greet(dev(zc, lax.rem(xc + r, 4), c))

    count = groups[...] * 4 - 3

    def keep(i):
        return jnp.where(i < count, 1.0, 0.0).astype(F32)

    zero_patch = jnp.zeros((K3, PIX), BF)
    sp[0:K3, :] = zero_patch
    sp[K3:2 * K3, :] = zero_patch
    sp[11 * K3:, :] = jnp.zeros((32, PIX), BF)
    xsp[0:K3, :] = zero_patch
    xsp[11 * HK:, :] = jnp.zeros((32, PIX), BF)
    dp_[0:K3, :] = zero_patch
    dp_[K3:2 * K3, :] = zero_patch
    pre[...] = jnp.zeros((C, PIX), F32)
    gain_b[...] = jnp.broadcast_to(gain[...], (PIX, C)).T
    gain_acc[...] = jnp.zeros((C, PIX), F32)
    col_sum[...] = jnp.zeros((8, N0 + N1), F32)
    acc0[...] = jnp.zeros((3, C, N0), F32)
    acc1[...] = jnp.zeros((3, C, N1), F32)

    def transpose_weight():
        for tap in range(27):
            to = (tap // 9) * 9 + 8 - tap % 9
            wt[:, to * C:(to + 1) * C] = weight[:, tap * C:(tap + 1) * C].T

    def own_weight():
        for t in range(3):
            for c in range(2):
                @pl.when(core == c)
                def _():
                    start = t * K3 + c * HK
                    whalf[t, :, 0:HK] = weight[:, start:start + HK]

            whalf[t, :, HK:] = jnp.zeros((C, N0 + N1 - HK), BF)
        lane = lax.broadcasted_iota(jnp.int32, (C, N0 + N1), 1) + HK * core
        channel = lax.broadcasted_iota(jnp.int32, (C, N0 + N1), 0)
        fold[...] = jnp.where(lax.rem(lane, C) == channel, 1.0, 0.0).astype(BF)

    @pl.when(seg == 0)
    def _():
        clip.wait()
        for i in range(F):
            xin[i] = (video_v[i].astype(F32) * keep(i)).astype(BF)

    early.wait()
    late.wait()

    @pl.when(seg >= 2)
    def _():
        transpose_weight()

    def fwd_copy(i):
        return put(feat.at[i], xin.at[i], fsend.at[i], frecv.at[i], {"segment": lax.rem(seg + 1, 4)})

    def bwd_copy(i):
        return put(dysend.at[i], dyin.at[i], bsend.at[i], brecv.at[i], {"segment": lax.rem(seg + 3, 4)})

    def keep_copy(i):
        return pltpu.make_async_copy(feat.at[i], feat_hbm.at[i], featsem.at[i])

    def pair_copy(i):
        src = pl.multiple_of((i + 2) * K3 + HK * (1 - core), 32)
        dst = pl.multiple_of((i + 2) * HK, 32)
        return put(sp.at[pl.ds(src, HK), :], xsp.at[pl.ds(dst, HK), :], psend.at[i], precv.at[i], dev(zc, xc, 1 - core))

    def dconv_copy(i):
        return put(dc.at[i], odc.at[i], csend.at[i], crecv.at[i], dev(zc, xc, 1 - core))

    def forward(i, carry):
        @pl.when(seg > 0)
        def _():
            fwd_copy(i).wait_recv()

        x = xin[i].astype(F32)
        scale = lax.rsqrt(jnp.sum(x * x, axis=0, keepdims=True) * (1.0 / C) + EPS)
        scales[i] = scale
        normed = (x * scale * gain_b[...]).astype(BF)
        patches = store_patches(sp, pl.multiple_of((i + 2) * K3, 64), normed)
        conv = pre[...] + jnp.dot(weight[:, 2 * K3:], patches, preferred_element_type=F32)
        sig = 1.0 / (1.0 + jnp.exp(-conv))
        feat[i] = ((x + conv * sig) * keep(i)).astype(BF)

        @pl.when(i == 0)
        def _():
            pl.semaphore_wait(barrier, 15)

        @pl.when(seg < 3)
        def _():
            fwd_copy(i).start()

        keep_copy(i).start()
        pair_copy(i).start()
        fac[i] = sig * (1.0 + conv * (1.0 - sig))
        window = sp[pl.ds(pl.multiple_of((i + 1) * K3, 64), 2 * K3), :]
        pre[...] = jnp.dot(weight[:, :2 * K3], window, preferred_element_type=F32)
        return carry

    lax.fori_loop(0, F, forward, 0)

    @pl.when(seg == 1)
    def _():
        transpose_weight()

    @pl.when(seg == 0)
    def _():
        own_weight()

    row = lax.broadcasted_iota(jnp.int32, (C, C), 0)
    colm = lax.broadcasted_iota(jnp.int32, (C, C), 1)
    blk = lax.div(row, 12)
    swapped = (lax.rem(blk, 4) * 4 + lax.div(blk, 4)) * 12 + lax.rem(row, 12)

    def z_first(h):
        return 1 - lax.rem(core + h, 2)

    def pick(h, first, second):
        return first * z_first(h) + second * (1 - z_first(h))

    def order(h):
        return jnp.where(colm == pick(h, row, swapped), 1.0, 0.0).astype(BF)

    def stage1(t, h, r):
        to = lax.rem(pick(h, zc, xc) + r, 4)
        where = {"dp": pick(h, to * 8 + xc * 2, zc * 8 + to * 2) + core}
        if h == 1:
            src, dst = c1.at[t, to], d1.at[t, r - 1]
        elif t < 2:
            src, dst = c0.at[t, to], d0.at[t, r - 1]
        else:
            src, dst = cg.at[to], dg.at[r - 1]
        return put(src, dst, s1send.at[t * 2 + h, r - 1], s1recv.at[t * 2 + h, r - 1], where)

    def emit(t, h, part):
        value = part.astype(BF)
        if t == 2 and h == 0:
            value = jnp.concatenate([value, gain_acc[...].astype(BF)], axis=1)
        rows = jnp.dot(order(h), value, preferred_element_type=F32).astype(BF)
        for q in range(4):
            if h == 1:
                c1[t, q] = rows[q * 48:(q + 1) * 48, :]
            elif t < 2:
                c0[t, q] = rows[q * 48:(q + 1) * 48, :]
            else:
                cg[q] = rows[q * 48:(q + 1) * 48, :]
        for r in (2, 1, 3):
            stage1(t, h, r).start()

    def add_columns(t):
        for acc, start, size in ((acc0, 0, N0), (acc1, N0, N1)):
            product = acc[t] * whalf[t, :, start:start + size].astype(F32)
            col_sum[:, start:start + size] += jnp.sum(product.reshape(C // 8, 8, size), axis=0)

    def gain_from_columns():
        sums = col_sum[...]
        high = sums.astype(BF)
        low = (sums - high.astype(F32)).astype(BF)
        both = jnp.concatenate([high, low], axis=0)
        per_channel = lax.dot_general(fold[...], both, NT, preferred_element_type=F32)
        gain_acc[:, 0:16] = per_channel / gain_b[:, 0:16]

    def patch_rows(t, i, start, size):
        own = pl.multiple_of((i + t) * K3 + HK * core + start, 32)
        other = pl.multiple_of((i + t) * HK + start, 32)
        return [sp[pl.ds(own, size), :], xsp[pl.ds(other, size), :]]

    def weight_product(t, frames, start, size):
        lhs, rhs = [], []
        for i in frames:
            lhs += [dc[i], odc[i]]
            rhs += patch_rows(t, i, start, size)
        return lax.dot_general(jnp.concatenate(lhs, axis=1), jnp.concatenate(rhs, axis=1), NT,
                               preferred_element_type=F32)

    pre[...] = jnp.zeros((C, PIX), F32)

    def wait_pairs():
        def body_(i, carry):
            pair_copy(i).wait_recv()
            return carry
        lax.fori_loop(0, F, body_, 0)

    @pl.when(seg == 3)
    def _():
        target.wait()

    def accumulate(t, i):
        acc0[t] += weight_product(t, [i], 0, N0)
        acc1[t] += weight_product(t, [i], N0, N1)

    def backward(n, carry):
        i = F - 1 - n

        @pl.when(seg < 3)
        def _():
            bwd_copy(i).wait_recv()

        dz = dyin[i].astype(F32) * keep(i)
        dconv = (dz * fac[i]).astype(BF)
        dc[i] = dconv
        patches = store_patches(dp_, pl.multiple_of((n + 2) * K3, 64), dconv)
        dnormed = pre[...] + jnp.dot(wt[:, 2 * K3:], patches, preferred_element_type=F32)
        x = xin[i].astype(F32)
        scale = scales[i]
        gx = dnormed * gain_b[...]
        inner = jnp.sum(gx * x, axis=0, keepdims=True)
        dx = scale * gx - x * (scale * scale * scale * inner * (1.0 / C)) + dz
        dysend[i] = dx.astype(BF)
        bwd_copy(i).start()
        dconv_copy(i).start()
        window = dp_[pl.ds(pl.multiple_of((n + 1) * K3, 64), 2 * K3), :]
        pre[...] = jnp.dot(wt[:, :2 * K3], window, preferred_element_type=F32)

        gain_acc[...] += dnormed * x * scale
        return carry

    @pl.when(seg > 0)
    def _():
        lax.fori_loop(0, F, backward, 0)
        wait_pairs()

        def arrived(i, carry):
            dconv_copy(i).wait_recv()
            return carry

        lax.fori_loop(0, F, arrived, 0)
        for t in range(3):
            frames = range(2 - t, F)
            emit(t, 0, weight_product(t, frames, 0, N0))
            emit(t, 1, weight_product(t, frames, N0, N1))

    def take(n):
        i = F - 1 - n
        bwd_copy(i).wait_recv()
        dconv = (dyin[i].astype(F32) * keep(i) * fac[i]).astype(BF)
        dc[i] = dconv
        dconv_copy(i).start()

    @pl.when(seg == 0)
    def _():
        wait_pairs()
        take(0)

        def step(n, carry):
            take(n)
            i = F - n
            dconv_copy(i).wait_recv()
            for t in range(3):
                accumulate(t, i)
            return carry

        lax.fori_loop(1, F - 1, step, 0)
        emit(0, 0, acc0[0])
        emit(0, 1, acc1[0])
        take(F - 1)
        dconv_copy(1).wait_recv()
        accumulate(1, 1)
        emit(1, 0, acc0[1])
        emit(1, 1, acc1[1])
        accumulate(2, 1)
        for t in range(2):
            add_columns(t)
        dconv_copy(0).wait_recv()
        accumulate(2, 0)
        emit(2, 1, acc1[2])
        add_columns(2)
        gain_from_columns()
        emit(2, 0, acc0[2])

    prow = lax.broadcasted_iota(jnp.int32, (64, 48), 0)
    pcol = lax.broadcasted_iota(jnp.int32, (64, 48), 1)
    spread = jnp.where((lax.rem(prow, 8) < 6) & (pcol == lax.div(prow, 8) * 6 + lax.rem(prow, 8)), 1.0, 0.0).astype(BF)

    def stage2(h, r, c):
        to = lax.rem(pick(h, xc, zc) + r, 4)
        where = {"dp": pick(h, zc * 8 + to * 2, to * 8 + xc * 2) + c}
        slot = r * 2 + jnp.where(c == core, 0, 1)
        src, dst = ((f0, g0), (f1, g1))[h]
        return put(src.at[to * 2 + c], dst.at[core * 4 + r], s2send.at[h, slot], s2recv.at[h, slot], where)

    def collect(own, got, out, start, size):
        total = own.astype(F32)
        for r in range(3):
            total = total + got[r].astype(F32)
        spaced = jnp.dot(spread, total.astype(BF), preferred_element_type=F32).astype(BF)
        for k in range(8):
            out[k, :, start:start + size] = spaced[k * 8:(k + 1) * 8, :]

    def finish_stage1(t, h):
        for r in range(1, 4):
            stage1(t, h, r).wait_recv()
        me = pick(h, zc, xc)
        if h == 1:
            collect(c1[t, me], d1[t], f1, t * N1, N1)
        elif t < 2:
            collect(c0[t, me], d0[t], f0, t * N0, N0)
        else:
            collect(cg[me], dg[...], f0, 2 * N0, N0 + PIX)

    def settle(i, carry):
        keep_copy(i).wait()
        pair_copy(i).wait_send()
        dconv_copy(i).wait_send()

        @pl.when(seg < 3)
        def _():
            fwd_copy(i).wait_send()

        @pl.when(seg > 0)
        def _():
            bwd_copy(i).wait_send()

        return carry

    for t in range(2):
        for h in range(2):
            finish_stage1(t, h)
    lax.fori_loop(0, F, settle, 0)
    for h in (1, 0):
        finish_stage1(2, h)
        for r in (2, 1, 3):
            stage2(h, r, core).start()
            stage2(h, r, 1 - core).start()
        stage2(h, 0, 1 - core).start()

    for r in range(1, 4):
        for t in range(3):
            stage1(t, 0, r).wait_send()
            stage1(t, 1, r).wait_send()

    def stage2_wait(h, r, c):
        slot = r * 2 + jnp.where(c == core, 0, 1)
        src, dst = ((f0, g0), (f1, g1))[h]
        return put(src.at[0], dst.at[c * 4 + r], s2send.at[h, slot], s2recv.at[h, slot], dev(zc, xc, 1 - core))

    for h in (1, 0):
        src, dst = ((f0, g0), (f1, g1))[h]
        dst[core * 4] = src[pick(h, xc, zc) * 2 + core]
        for r in range(4):
            if r:
                stage2_wait(h, r, core).wait_recv()
            stage2_wait(h, r, 1 - core).wait_recv()
        for c in range(2):
            total = dst[c * 4].astype(F32)
            for r in range(1, 4):
                total = total + dst[c * 4 + r].astype(F32)
            if h == 0:
                per_row = jnp.sum(total[:, 3 * N0:], axis=1, keepdims=True)
                gain_rows = per_row if c == 0 else gain_rows + per_row
            for t in range(3):
                start = t * K3 + c * HK + (0 if h == 0 else N0)
                size = N0 if h == 0 else HK - N0
                first = t * (N0 if h == 0 else N1)
                for j in range(6):
                    dweight[j, :, start:start + size] = total[j:j + 1, first:first + size]

    r8 = lax.broadcasted_iota(jnp.int32, (8, 128), 0)
    l8 = lax.broadcasted_iota(jnp.int32, (8, 128), 1)
    dgain[...] = jnp.sum(jnp.where(r8 == l8, gain_rows, 0.0), axis=0, keepdims=True)

    results = (pltpu.make_async_copy(dweight, dweight_hbm, outsem.at[0]),
               pltpu.make_async_copy(dgain, dgain_hbm, outsem.at[1]))
    for result in results:
        result.start()

    for h in range(2):
        for r in range(4):
            if r:
                stage2_wait(h, r, core).wait_send()
            stage2_wait(h, r, 1 - core).wait_send()
    for result in results:
        result.wait()


def hand_over(feat, dweight, dgain, feat_out, dweight_out, dgain_out):
    feat_out[...] = feat[...]
    dweight_out[...] = dweight[...]
    dgain_out[...] = dgain[:, 0:6]


def body(video_clips, conv_weight, norm_gain, cotangent, clip_groups):
    vmem = pl.BlockSpec(memory_space=pltpu.VMEM)
    hbm = pl.BlockSpec(memory_space=pl.ANY)
    dma = pltpu.SemaphoreType.DMA
    feat, dweight, dgain = pl.pallas_call(
        kernel,
        out_shape=(
            jax.ShapeDtypeStruct((F, C, PIX), BF),
            jax.ShapeDtypeStruct((6, 1, KK), F32),
            jax.ShapeDtypeStruct((1, 128), F32),
        ),
        in_specs=[vmem, hbm, hbm, vmem, hbm],
        out_specs=(hbm, hbm, hbm),
        scratch_shapes=[
            pltpu.VMEM((C, KK), BF),
            pltpu.VMEM((F, C, PIX), BF),
            pltpu.VMEM((F, C, PIX), BF),
            pltpu.VMEM((6, 1, KK), F32),
            pltpu.VMEM((1, 128), F32),
            pltpu.VMEM((C, PIX), F32),
            pltpu.VMEM((F, C, PIX), BF),
            pltpu.VMEM((F, C, PIX), BF),
            pltpu.VMEM((F, C, PIX), BF),
            pltpu.VMEM((F, C, PIX), F32),
            pltpu.VMEM((F, 1, PIX), F32),
            pltpu.VMEM((C, PIX), F32),
            pltpu.VMEM((C, PIX), F32),
            pltpu.VMEM((11 * K3 + 32, PIX), BF),
            pltpu.VMEM((11 * HK + 32, PIX), BF),
            pltpu.VMEM((11 * K3, PIX), BF),
            pltpu.VMEM((C, KK), BF),
            pltpu.VMEM((3, C, N0 + N1), BF),
            pltpu.VMEM((C, N0 + N1), BF),
            pltpu.VMEM((F, C, PIX), BF),
            pltpu.VMEM((F, C, PIX), BF),
            pltpu.VMEM((3, C, N0), F32),
            pltpu.VMEM((3, C, N1), F32),
            pltpu.VMEM((8, N0 + N1), F32),
            pltpu.VMEM((2, 4, 48, N0), BF),
            pltpu.VMEM((3, 4, 48, N1), BF),
            pltpu.VMEM((4, 48, N0 + PIX), BF),
            pltpu.VMEM((2, 3, 48, N0), BF),
            pltpu.VMEM((3, 3, 48, N1), BF),
            pltpu.VMEM((3, 48, N0 + PIX), BF),
            pltpu.VMEM((8, 8, 3 * N0 + PIX), BF),
            pltpu.VMEM((8, 8, 3 * N1), BF),
            pltpu.VMEM((8, 8, 3 * N0 + PIX), BF),
            pltpu.VMEM((8, 8, 3 * N1), BF),
            dma((3,)), dma((2,)), dma((F,)),
            dma((F,)), dma((F,)), dma((F,)), dma((F,)),
            dma((F,)), dma((F,)), dma((F,)), dma((F,)),
            dma((6, 3)), dma((6, 3)),
            dma((2, 8)), dma((2, 8)),
        ],
        compiler_params=pltpu.CompilerParams(
            collective_id=0, has_side_effects=True, vmem_limit_bytes=56 << 20),
    )(clip_groups.reshape(1, 1), video_clips[0], conv_weight[0], norm_gain, cotangent[0])
    feat, dweight, dgain = pl.pallas_call(
        hand_over,
        out_shape=(
            jax.ShapeDtypeStruct((F, C, PIX), BF),
            jax.ShapeDtypeStruct((6, 1, KK), F32),
            jax.ShapeDtypeStruct((1, 6), F32),
        ),
        in_specs=[vmem, vmem, vmem],
        out_specs=(vmem, vmem, vmem),
    )(feat, dweight, dgain)
    return (feat[None, None], jnp.transpose(dweight, (1, 0, 2)), dgain)


def solution(mesh):
    placed = (
        P("dp", None, None, None),
        P("segment", None, None),
        P("segment", None),
        P("dp", None, None, None),
        P("dp"),
    )
    return jax.shard_map(
        body,
        mesh=mesh,
        in_specs=placed,
        out_specs=(
            P("segment", "dp", None, None, None),
            P("segment", "dp", None),
            P("segment", "dp"),
        ),
        check_vma=False,
    )
```

```python
import jax
import jax.numpy as jnp
from jax import lax
from jax.experimental import pallas as pl
from jax.experimental.pallas import tpu as pltpu
from jax.sharding import PartitionSpec as P

TILE_H = 8
TILE_W = 16
EPS = 1e-06

F = 9
C = 192
PIX = 128
K3 = 9 * C
KK = 27 * C
HK = K3 // 2
N0 = 512
N1 = 384

BF = jnp.bfloat16
F32 = jnp.float32
NT = (((1,), (1,)), ((), ()))


def tap_masks():
    lane = lax.broadcasted_iota(jnp.int32, (1, PIX), 1)
    col = lane & (TILE_W - 1)
    masks = []
    for a in range(3):
        for b in range(3):
            pos = lane + TILE_W * (a - 1)
            ok = (col + (b - 1) >= 0) & (col + (b - 1) < TILE_W) & (pos >= 0) & (pos < PIX)
            masks.append(jnp.where(ok, 1.0, 0.0).astype(BF))
    return masks


def store_patches(dst, base, frame):
    masks = tap_masks()
    values = []
    for a in range(3):
        for b in range(3):
            k = a * 3 + b
            shift = (-(TILE_W * (a - 1) + (b - 1))) % PIX
            values.append(frame if shift == 0 else pltpu.roll(frame, shift, 1) * masks[k])
    patches = jnp.concatenate(values, axis=0)
    dst[pl.ds(base, K3), :] = patches
    return patches


def kernel(groups, video, weight_hbm, gain_hbm, cot, feat_hbm, dweight_hbm, dgain_hbm,
           gain, weight, feat, video_v, dweight, dgain, pre, xin, dyin, dysend, fac, scales, gain_b, gain_acc,
           sp, xsp, dp_, wt, whalf, fold, dc, odc, acc0, acc1, col_sum,
           c0, c1, cg, d0, d1, dg, f0, f1, g0, g1,
           insem, outsem, featsem, fsend, frecv, bsend, brecv, psend, precv, csend, crecv,
           s1send, s1recv, s2send, s2recv):
    seg = lax.axis_index("segment")
    d = lax.axis_index("dp")
    core = lax.rem(d, 2)
    xc = lax.rem(lax.div(d, 2), 4)
    zc = lax.div(d, 8)

    def dev(z, x, c):
        return {"dp": (z * 4 + x) * 2 + c}

    def put(src, dst, ssem, rsem, where):
        return pltpu.make_async_remote_copy(
            src_ref=src, dst_ref=dst, send_sem=ssem, recv_sem=rsem,
            device_id=where, device_id_type=pl.DeviceIdType.MESH)

    barrier = pltpu.get_barrier_semaphore()

    def greet(where):
        pl.semaphore_signal(barrier, inc=1, device_id=where, device_id_type=pl.DeviceIdType.MESH)

    greet({"segment": lax.rem(seg + 1, 4)})
    greet({"segment": lax.rem(seg + 3, 4)})
    greet(dev(zc, xc, 1 - core))
    for r in range(1, 4):
        for c in range(2):
            greet(dev(lax.rem(zc + r, 4), xc, c))
            greet(dev(zc, lax.rem(xc + r, 4), c))

    early = pltpu.make_async_copy(weight_hbm.at[:, 2 * K3:], weight.at[:, 2 * K3:], insem.at[0])
    late = pltpu.make_async_copy(weight_hbm.at[:, :2 * K3], weight.at[:, :2 * K3], insem.at[1])
    clip = pltpu.make_async_copy(video, video_v, insem.at[2])
    target = pltpu.make_async_copy(cot, dyin, insem.at[2])

    @pl.when(seg == 0)
    def _():
        clip.start()

    gains = pltpu.make_async_copy(gain_hbm, gain, insem.at[3])
    gains.start()
    early.start()
    late.start()

    @pl.when(seg == 3)
    def _():
        target.start()

    count = groups[...].reshape(1, 1) * 4 - 3

    def keep(i):
        return jnp.where(i < count, 1.0, 0.0).astype(F32)

    zero_patch = jnp.zeros((K3, PIX), BF)
    sp[0:K3, :] = zero_patch
    sp[K3:2 * K3, :] = zero_patch
    sp[11 * K3:, :] = jnp.zeros((32, PIX), BF)
    xsp[0:K3, :] = zero_patch
    xsp[11 * HK:, :] = jnp.zeros((32, PIX), BF)
    dp_[0:K3, :] = zero_patch
    dp_[K3:2 * K3, :] = zero_patch
    pre[...] = jnp.zeros((C, PIX), F32)
    gains.wait()
    gain_b[...] = jnp.broadcast_to(gain[...], (PIX, C)).T
    gain_acc[...] = jnp.zeros((C, PIX), F32)
    col_sum[...] = jnp.zeros((8, N0 + N1), F32)
    acc0[...] = jnp.zeros((3, C, N0), F32)
    acc1[...] = jnp.zeros((3, C, N1), F32)

    def transpose_weight():
        for tap in range(27):
            to = (tap // 9) * 9 + 8 - tap % 9
            wt[:, to * C:(to + 1) * C] = weight[:, tap * C:(tap + 1) * C].T

    def own_weight():
        for t in range(3):
            for c in range(2):
                @pl.when(core == c)
                def _():
                    start = t * K3 + c * HK
                    whalf[t, :, 0:HK] = weight[:, start:start + HK]

            whalf[t, :, HK:] = jnp.zeros((C, N0 + N1 - HK), BF)
        lane = lax.broadcasted_iota(jnp.int32, (C, N0 + N1), 1) + HK * core
        channel = lax.broadcasted_iota(jnp.int32, (C, N0 + N1), 0)
        fold[...] = jnp.where(lax.rem(lane, C) == channel, 1.0, 0.0).astype(BF)

    @pl.when(seg == 0)
    def _():
        clip.wait()
        for i in range(F):
            xin[i] = (video_v[i].astype(F32) * keep(i)).astype(BF)

    early.wait()
    late.wait()

    @pl.when(seg >= 2)
    def _():
        transpose_weight()

    def fwd_copy(i):
        return put(feat.at[i], xin.at[i], fsend.at[i], frecv.at[i], {"segment": lax.rem(seg + 1, 4)})

    def bwd_copy(i):
        return put(dysend.at[i], dyin.at[i], bsend.at[i], brecv.at[i], {"segment": lax.rem(seg + 3, 4)})

    def keep_copy(i):
        return pltpu.make_async_copy(feat.at[i], feat_hbm.at[i], featsem.at[i])

    def pair_copy(i):
        src = pl.multiple_of((i + 2) * K3 + HK * (1 - core), 32)
        dst = pl.multiple_of((i + 2) * HK, 32)
        return put(sp.at[pl.ds(src, HK), :], xsp.at[pl.ds(dst, HK), :], psend.at[i], precv.at[i], dev(zc, xc, 1 - core))

    def dconv_copy(i):
        return put(dc.at[i], odc.at[i], csend.at[i], crecv.at[i], dev(zc, xc, 1 - core))

    def forward(i, carry):
        @pl.when(seg > 0)
        def _():
            fwd_copy(i).wait_recv()

        x = xin[i].astype(F32)
        scale = lax.rsqrt(jnp.sum(x * x, axis=0, keepdims=True) * (1.0 / C) + EPS)
        scales[i] = scale
        normed = (x * scale * gain_b[...]).astype(BF)
        patches = store_patches(sp, pl.multiple_of((i + 2) * K3, 64), normed)
        conv = pre[...] + jnp.dot(weight[:, 2 * K3:], patches, preferred_element_type=F32)
        sig = 1.0 / (1.0 + jnp.exp(-conv))
        feat[i] = ((x + conv * sig) * keep(i)).astype(BF)

        @pl.when(i == 0)
        def _():
            pl.semaphore_wait(barrier, 15)

        @pl.when(seg < 3)
        def _():
            fwd_copy(i).start()

        keep_copy(i).start()
        pair_copy(i).start()
        fac[i] = sig * (1.0 + conv * (1.0 - sig))

        @pl.when(i < F - 1)
        def _():
            window = sp[pl.ds(pl.multiple_of((i + 1) * K3, 64), 2 * K3), :]
            pre[...] = jnp.dot(weight[:, :2 * K3], window, preferred_element_type=F32)

        return carry

    lax.fori_loop(0, F, forward, 0)

    @pl.when(seg == 1)
    def _():
        transpose_weight()

    @pl.when(seg == 0)
    def _():
        own_weight()

    row = lax.broadcasted_iota(jnp.int32, (C, C), 0)
    colm = lax.broadcasted_iota(jnp.int32, (C, C), 1)
    blk = lax.div(row, 12)
    swapped = (lax.rem(blk, 4) * 4 + lax.div(blk, 4)) * 12 + lax.rem(row, 12)

    def z_first(h):
        return 1 - lax.rem(core + h, 2)

    def pick(h, first, second):
        return first * z_first(h) + second * (1 - z_first(h))

    def order(h):
        return jnp.where(colm == pick(h, row, swapped), 1.0, 0.0).astype(BF)

    def stage1(t, h, r):
        to = lax.rem(pick(h, zc, xc) + r, 4)
        where = {"dp": pick(h, to * 8 + xc * 2, zc * 8 + to * 2) + core}
        if h == 1:
            src, dst = c1.at[t, to], d1.at[t, r - 1]
        elif t < 2:
            src, dst = c0.at[t, to], d0.at[t, r - 1]
        else:
            src, dst = cg.at[to], dg.at[r - 1]
        return put(src, dst, s1send.at[t * 2 + h, r - 1], s1recv.at[t * 2 + h, r - 1], where)

    def emit(t, h, part):
        value = part.astype(BF)
        if t == 2 and h == 0:
            value = jnp.concatenate([value, gain_acc[...].astype(BF)], axis=1)
        rows = jnp.dot(order(h), value, preferred_element_type=F32).astype(BF)
        for q in range(4):
            if h == 1:
                c1[t, q] = rows[q * 48:(q + 1) * 48, :]
            elif t < 2:
                c0[t, q] = rows[q * 48:(q + 1) * 48, :]
            else:
                cg[q] = rows[q * 48:(q + 1) * 48, :]
        for r in (2, 1, 3):
            stage1(t, h, r).start()

    def add_columns(t):
        for acc, start, size in ((acc0, 0, N0), (acc1, N0, N1)):
            product = acc[t] * whalf[t, :, start:start + size].astype(F32)
            col_sum[:, start:start + size] += jnp.sum(product.reshape(C // 8, 8, size), axis=0)

    def gain_from_columns():
        sums = col_sum[...]
        high = sums.astype(BF)
        low = (sums - high.astype(F32)).astype(BF)
        both = jnp.concatenate([high, low], axis=0)
        per_channel = lax.dot_general(fold[...], both, NT, preferred_element_type=F32)
        gain_acc[:, 0:16] = per_channel / gain_b[:, 0:16]

    def patch_rows(t, i, start, size):
        own = pl.multiple_of((i + t) * K3 + HK * core + start, 32)
        other = pl.multiple_of((i + t) * HK + start, 32)
        return [sp[pl.ds(own, size), :], xsp[pl.ds(other, size), :]]

    def weight_product(t, frames, start, size):
        lhs, rhs = [], []
        for i in frames:
            lhs += [dc[i], odc[i]]
            rhs += patch_rows(t, i, start, size)
        return lax.dot_general(jnp.concatenate(lhs, axis=1), jnp.concatenate(rhs, axis=1), NT,
                               preferred_element_type=F32)

    pre[...] = jnp.zeros((C, PIX), F32)

    def wait_pairs():
        def body_(i, carry):
            pair_copy(i).wait_recv()
            return carry
        lax.fori_loop(0, F, body_, 0)

    @pl.when(seg == 3)
    def _():
        target.wait()

    def accumulate(t, i):
        acc0[t] += weight_product(t, [i], 0, N0)
        acc1[t] += weight_product(t, [i], N0, N1)

    def backward(n, carry):
        i = F - 1 - n

        @pl.when(seg < 3)
        def _():
            bwd_copy(i).wait_recv()

        dz = dyin[i].astype(F32) * keep(i)
        dconv = (dz * fac[i]).astype(BF)
        dc[i] = dconv
        patches = store_patches(dp_, pl.multiple_of((n + 2) * K3, 64), dconv)
        dnormed = pre[...] + jnp.dot(wt[:, 2 * K3:], patches, preferred_element_type=F32)
        x = xin[i].astype(F32)
        scale = scales[i]
        gx = dnormed * gain_b[...]
        inner = jnp.sum(gx * x, axis=0, keepdims=True)
        dx = scale * gx - x * (scale * scale * scale * inner * (1.0 / C)) + dz
        dysend[i] = dx.astype(BF)
        bwd_copy(i).start()
        dconv_copy(i).start()
        gain_acc[...] += dnormed * x * scale

        @pl.when(n < F - 1)
        def _():
            window = dp_[pl.ds(pl.multiple_of((n + 1) * K3, 64), 2 * K3), :]
            pre[...] = jnp.dot(wt[:, :2 * K3], window, preferred_element_type=F32)

        return carry

    @pl.when(seg > 0)
    def _():
        lax.fori_loop(0, F, backward, 0)
        wait_pairs()

        def arrived(i, carry):
            dconv_copy(i).wait_recv()
            return carry

        lax.fori_loop(0, F, arrived, 0)
        for t in range(3):
            frames = range(2 - t, F)
            emit(t, 0, weight_product(t, frames, 0, N0))
            emit(t, 1, weight_product(t, frames, N0, N1))

    def take(n):
        i = F - 1 - n
        bwd_copy(i).wait_recv()
        dconv = (dyin[i].astype(F32) * keep(i) * fac[i]).astype(BF)
        dc[i] = dconv
        dconv_copy(i).start()

    @pl.when(seg == 0)
    def _():
        wait_pairs()
        take(0)

        def step(n, carry):
            take(n)
            i = F - n
            dconv_copy(i).wait_recv()
            for t in range(3):
                accumulate(t, i)
            return carry

        lax.fori_loop(1, F - 1, step, 0)
        emit(0, 0, acc0[0])
        emit(0, 1, acc1[0])
        take(F - 1)
        dconv_copy(1).wait_recv()
        accumulate(1, 1)
        emit(1, 0, acc0[1])
        emit(1, 1, acc1[1])
        accumulate(2, 1)
        for t in range(2):
            add_columns(t)
        dconv_copy(0).wait_recv()
        accumulate(2, 0)
        emit(2, 1, acc1[2])
        add_columns(2)
        gain_from_columns()
        emit(2, 0, acc0[2])

    prow = lax.broadcasted_iota(jnp.int32, (64, 48), 0)
    pcol = lax.broadcasted_iota(jnp.int32, (64, 48), 1)
    spread = jnp.where((lax.rem(prow, 8) < 6) & (pcol == lax.div(prow, 8) * 6 + lax.rem(prow, 8)), 1.0, 0.0).astype(BF)

    def stage2(h, r, c):
        to = lax.rem(pick(h, xc, zc) + r, 4)
        where = {"dp": pick(h, zc * 8 + to * 2, to * 8 + xc * 2) + c}
        slot = r * 2 + jnp.where(c == core, 0, 1)
        src, dst = ((f0, g0), (f1, g1))[h]
        return put(src.at[to * 2 + c], dst.at[core * 4 + r], s2send.at[h, slot], s2recv.at[h, slot], where)

    def collect(own, got, out, start, size):
        total = own.astype(F32)
        for r in range(3):
            total = total + got[r].astype(F32)
        spaced = jnp.dot(spread, total.astype(BF), preferred_element_type=F32).astype(BF)
        for k in range(8):
            out[k, :, start:start + size] = spaced[k * 8:(k + 1) * 8, :]

    def finish_stage1(t, h):
        for r in range(1, 4):
            stage1(t, h, r).wait_recv()
        me = pick(h, zc, xc)
        if h == 1:
            collect(c1[t, me], d1[t], f1, t * N1, N1)
        elif t < 2:
            collect(c0[t, me], d0[t], f0, t * N0, N0)
        else:
            collect(cg[me], dg[...], f0, 2 * N0, N0 + PIX)

    def settle(i, carry):
        keep_copy(i).wait()
        pair_copy(i).wait_send()
        dconv_copy(i).wait_send()

        @pl.when(seg < 3)
        def _():
            fwd_copy(i).wait_send()

        @pl.when(seg > 0)
        def _():
            bwd_copy(i).wait_send()

        return carry

    for t in range(2):
        for h in range(2):
            finish_stage1(t, h)
    lax.fori_loop(0, F, settle, 0)
    for h in (1, 0):
        finish_stage1(2, h)
        for r in (2, 1, 3):
            stage2(h, r, core).start()
            stage2(h, r, 1 - core).start()
        stage2(h, 0, 1 - core).start()

    for r in range(1, 4):
        for t in range(3):
            stage1(t, 0, r).wait_send()
            stage1(t, 1, r).wait_send()

    def stage2_wait(h, r, c):
        slot = r * 2 + jnp.where(c == core, 0, 1)
        src, dst = ((f0, g0), (f1, g1))[h]
        return put(src.at[0], dst.at[c * 4 + r], s2send.at[h, slot], s2recv.at[h, slot], dev(zc, xc, 1 - core))

    for h in (1, 0):
        src, dst = ((f0, g0), (f1, g1))[h]
        dst[core * 4] = src[pick(h, xc, zc) * 2 + core]
        for r in range(4):
            if r:
                stage2_wait(h, r, core).wait_recv()
            stage2_wait(h, r, 1 - core).wait_recv()
        for c in range(2):
            total = dst[c * 4].astype(F32)
            for r in range(1, 4):
                total = total + dst[c * 4 + r].astype(F32)
            if h == 0:
                per_row = jnp.sum(total[:, 3 * N0:], axis=1, keepdims=True)
                gain_rows = per_row if c == 0 else gain_rows + per_row
            for t in range(3):
                start = t * K3 + c * HK + (0 if h == 0 else N0)
                size = N0 if h == 0 else HK - N0
                first = t * (N0 if h == 0 else N1)
                for j in range(6):
                    dweight[j, :, start:start + size] = total[j:j + 1, first:first + size]

    r8 = lax.broadcasted_iota(jnp.int32, (8, 128), 0)
    l8 = lax.broadcasted_iota(jnp.int32, (8, 128), 1)
    dgain[...] = jnp.sum(jnp.where(r8 == l8, gain_rows, 0.0), axis=0, keepdims=True)

    results = (pltpu.make_async_copy(dweight, dweight_hbm, outsem.at[0]),
               pltpu.make_async_copy(dgain, dgain_hbm, outsem.at[1]))
    for result in results:
        result.start()

    for h in range(2):
        for r in range(4):
            if r:
                stage2_wait(h, r, core).wait_send()
            stage2_wait(h, r, 1 - core).wait_send()
    for result in results:
        result.wait()


def hand_over(feat, dweight, dgain, feat_out, dweight_out, dgain_out, sems):
    copies = (pltpu.make_async_copy(feat, feat_out, sems.at[0]),
              pltpu.make_async_copy(dweight, dweight_out, sems.at[1]))
    for copy in copies:
        copy.start()
    dgain_out[...] = dgain[:, 0:6]
    for copy in copies:
        copy.wait()


def body(video_clips, conv_weight, norm_gain, cotangent, clip_groups):
    vmem = pl.BlockSpec(memory_space=pltpu.VMEM)
    hbm = pl.BlockSpec(memory_space=pl.ANY)
    dma = pltpu.SemaphoreType.DMA
    feat, dweight, dgain = pl.pallas_call(
        kernel,
        out_shape=(
            jax.ShapeDtypeStruct((F, C, PIX), BF),
            jax.ShapeDtypeStruct((6, 1, KK), F32),
            jax.ShapeDtypeStruct((1, 128), F32),
        ),
        in_specs=[vmem, hbm, hbm, hbm, hbm],
        out_specs=(hbm, hbm, hbm),
        scratch_shapes=[
            pltpu.VMEM((1, C), F32),
            pltpu.VMEM((C, KK), BF),
            pltpu.VMEM((F, C, PIX), BF),
            pltpu.VMEM((F, C, PIX), BF),
            pltpu.VMEM((6, 1, KK), F32),
            pltpu.VMEM((1, 128), F32),
            pltpu.VMEM((C, PIX), F32),
            pltpu.VMEM((F, C, PIX), BF),
            pltpu.VMEM((F, C, PIX), BF),
            pltpu.VMEM((F, C, PIX), BF),
            pltpu.VMEM((F, C, PIX), F32),
            pltpu.VMEM((F, 1, PIX), F32),
            pltpu.VMEM((C, PIX), F32),
            pltpu.VMEM((C, PIX), F32),
            pltpu.VMEM((11 * K3 + 32, PIX), BF),
            pltpu.VMEM((11 * HK + 32, PIX), BF),
            pltpu.VMEM((11 * K3, PIX), BF),
            pltpu.VMEM((C, KK), BF),
            pltpu.VMEM((3, C, N0 + N1), BF),
            pltpu.VMEM((C, N0 + N1), BF),
            pltpu.VMEM((F, C, PIX), BF),
            pltpu.VMEM((F, C, PIX), BF),
            pltpu.VMEM((3, C, N0), F32),
            pltpu.VMEM((3, C, N1), F32),
            pltpu.VMEM((8, N0 + N1), F32),
            pltpu.VMEM((2, 4, 48, N0), BF),
            pltpu.VMEM((3, 4, 48, N1), BF),
            pltpu.VMEM((4, 48, N0 + PIX), BF),
            pltpu.VMEM((2, 3, 48, N0), BF),
            pltpu.VMEM((3, 3, 48, N1), BF),
            pltpu.VMEM((3, 48, N0 + PIX), BF),
            pltpu.VMEM((8, 8, 3 * N0 + PIX), BF),
            pltpu.VMEM((8, 8, 3 * N1), BF),
            pltpu.VMEM((8, 8, 3 * N0 + PIX), BF),
            pltpu.VMEM((8, 8, 3 * N1), BF),
            dma((4,)), dma((2,)), dma((F,)),
            dma((F,)), dma((F,)), dma((F,)), dma((F,)),
            dma((F,)), dma((F,)), dma((F,)), dma((F,)),
            dma((6, 3)), dma((6, 3)),
            dma((2, 8)), dma((2, 8)),
        ],
        compiler_params=pltpu.CompilerParams(
            collective_id=0, has_side_effects=True, vmem_limit_bytes=36 << 20),
    )(clip_groups, *(pltpu.with_memory_space_constraint(v, pltpu.HBM) for v in (video_clips[0], conv_weight[0])), pltpu.with_memory_space_constraint(norm_gain, pltpu.HBM), pltpu.with_memory_space_constraint(cotangent[0], pltpu.HBM))
    feat, dweight, dgain = pl.pallas_call(
        hand_over,
        out_shape=(
            jax.ShapeDtypeStruct((F, C, PIX), BF),
            jax.ShapeDtypeStruct((6, 1, KK), F32),
            jax.ShapeDtypeStruct((1, 6), F32),
        ),
        in_specs=[hbm, hbm, vmem],
        out_specs=(hbm, hbm, vmem),
        scratch_shapes=[dma((2,))],
        compiler_params=pltpu.CompilerParams(vmem_limit_bytes=4 << 20),
    )(feat, dweight, dgain)
    return (feat[None, None], jnp.transpose(dweight, (1, 0, 2)), dgain)


def solution(mesh):
    placed = (
        P("dp", None, None, None),
        P("segment", None, None),
        P("segment", None),
        P("dp", None, None, None),
        P("dp"),
    )
    return jax.shard_map(
        body,
        mesh=mesh,
        in_specs=placed,
        out_specs=(
            P("segment", "dp", None, None, None),
            P("segment", "dp", None),
            P("segment", "dp"),
        ),
        check_vma=False,
    )
```

```python
import jax
import jax.numpy as jnp
from jax import lax
from jax.experimental import pallas as pl
from jax.experimental.pallas import tpu as pltpu
from jax.sharding import PartitionSpec as P

TILE_H = 8
TILE_W = 16
EPS = 1e-06

F = 9
C = 192
PIX = 128
K3 = 9 * C
KK = 27 * C
HK = K3 // 2
N0 = 512
N1 = 384

BF = jnp.bfloat16
F32 = jnp.float32
NT = (((1,), (1,)), ((), ()))


def tap_masks():
    lane = lax.broadcasted_iota(jnp.int32, (1, PIX), 1)
    col = lane & (TILE_W - 1)
    masks = []
    for a in range(3):
        for b in range(3):
            pos = lane + TILE_W * (a - 1)
            ok = (col + (b - 1) >= 0) & (col + (b - 1) < TILE_W) & (pos >= 0) & (pos < PIX)
            masks.append(jnp.where(ok, 1.0, 0.0).astype(BF))
    return masks


def store_patches(dst, base, frame):
    masks = tap_masks()
    values = []
    for a in range(3):
        for b in range(3):
            k = a * 3 + b
            shift = (-(TILE_W * (a - 1) + (b - 1))) % PIX
            values.append(frame if shift == 0 else pltpu.roll(frame, shift, 1) * masks[k])
    patches = jnp.concatenate(values, axis=0)
    dst[pl.ds(base, K3), :] = patches
    return patches


def kernel(groups, video, weight_hbm, gain_hbm, cot, feat, dweight, dgain,
           gain, weight, video_v, pre, xin, dyin, dysend, fac, scales, gain_b, gain_acc,
           sp, xsp, dp_, wt, whalf, fold, dc, odc, acc0, acc1, col_sum,
           c0, c1, cg, d0, d1, dg, f0, f1, g0, g1,
           insem, fsend, frecv, bsend, brecv, psend, precv, csend, crecv,
           s1send, s1recv, s2send, s2recv):
    seg = lax.axis_index("segment")
    d = lax.axis_index("dp")
    core = lax.rem(d, 2)
    xc = lax.rem(lax.div(d, 2), 4)
    zc = lax.div(d, 8)

    def dev(z, x, c):
        return {"dp": (z * 4 + x) * 2 + c}

    def put(src, dst, ssem, rsem, where):
        return pltpu.make_async_remote_copy(
            src_ref=src, dst_ref=dst, send_sem=ssem, recv_sem=rsem,
            device_id=where, device_id_type=pl.DeviceIdType.MESH)

    barrier = pltpu.get_barrier_semaphore()

    def greet(where):
        pl.semaphore_signal(barrier, inc=1, device_id=where, device_id_type=pl.DeviceIdType.MESH)

    greet({"segment": lax.rem(seg + 1, 4)})
    greet({"segment": lax.rem(seg + 3, 4)})
    greet(dev(zc, xc, 1 - core))
    for r in range(1, 4):
        for c in range(2):
            greet(dev(lax.rem(zc + r, 4), xc, c))
            greet(dev(zc, lax.rem(xc + r, 4), c))

    early = pltpu.make_async_copy(weight_hbm.at[:, 2 * K3:], weight.at[:, 2 * K3:], insem.at[0])
    late = pltpu.make_async_copy(weight_hbm.at[:, :2 * K3], weight.at[:, :2 * K3], insem.at[1])
    clip = pltpu.make_async_copy(video, video_v, insem.at[2])
    target = pltpu.make_async_copy(cot, dyin, insem.at[2])

    @pl.when(seg == 0)
    def _():
        clip.start()

    gains = pltpu.make_async_copy(gain_hbm, gain, insem.at[3])
    gains.start()
    early.start()
    late.start()

    @pl.when(seg == 3)
    def _():
        target.start()

    count = groups[...].reshape(1, 1) * 4 - 3

    def keep(i):
        return jnp.where(i < count, 1.0, 0.0).astype(F32)

    zero_patch = jnp.zeros((K3, PIX), BF)
    sp[0:K3, :] = zero_patch
    sp[K3:2 * K3, :] = zero_patch
    sp[11 * K3:, :] = jnp.zeros((32, PIX), BF)
    xsp[0:K3, :] = zero_patch
    xsp[11 * HK:, :] = jnp.zeros((32, PIX), BF)
    dp_[0:K3, :] = zero_patch
    dp_[K3:2 * K3, :] = zero_patch
    pre[...] = jnp.zeros((C, PIX), F32)
    gains.wait()
    gain_b[...] = jnp.broadcast_to(gain[...], (PIX, C)).T
    gain_acc[...] = jnp.zeros((C, PIX), F32)
    col_sum[...] = jnp.zeros((8, N0 + N1), F32)
    acc0[...] = jnp.zeros((3, C, N0), F32)
    acc1[...] = jnp.zeros((3, C, N1), F32)

    def transpose_weight():
        for tap in range(27):
            to = (tap // 9) * 9 + 8 - tap % 9
            wt[:, to * C:(to + 1) * C] = weight[:, tap * C:(tap + 1) * C].T

    def own_weight():
        for t in range(3):
            for c in range(2):
                @pl.when(core == c)
                def _():
                    start = t * K3 + c * HK
                    whalf[t, :, 0:HK] = weight[:, start:start + HK]

            whalf[t, :, HK:] = jnp.zeros((C, N0 + N1 - HK), BF)
        lane = lax.broadcasted_iota(jnp.int32, (C, N0 + N1), 1) + HK * core
        channel = lax.broadcasted_iota(jnp.int32, (C, N0 + N1), 0)
        fold[...] = jnp.where(lax.rem(lane, C) == channel, 1.0, 0.0).astype(BF)

    @pl.when(seg == 0)
    def _():
        clip.wait()
        for i in range(F):
            xin[i] = (video_v[i].astype(F32) * keep(i)).astype(BF)

    early.wait()
    late.wait()

    @pl.when((seg == 0) & (core == 1))
    def _():
        own_weight()

    @pl.when(seg >= 2)
    def _():
        transpose_weight()

    def fwd_copy(i):
        return put(feat.at[i], xin.at[i], fsend.at[i], frecv.at[i], {"segment": lax.rem(seg + 1, 4)})

    def bwd_copy(i):
        return put(dysend.at[i], dyin.at[i], bsend.at[i], brecv.at[i], {"segment": lax.rem(seg + 3, 4)})

    def pair_copy(i):
        src = pl.multiple_of((i + 2) * K3 + HK * (1 - core), 32)
        dst = pl.multiple_of((i + 2) * HK, 32)
        return put(sp.at[pl.ds(src, HK), :], xsp.at[pl.ds(dst, HK), :], psend.at[i], precv.at[i], dev(zc, xc, 1 - core))

    def dconv_copy(i):
        return put(dc.at[i], odc.at[i], csend.at[i], crecv.at[i], dev(zc, xc, 1 - core))

    def forward(i, carry):
        @pl.when(seg > 0)
        def _():
            fwd_copy(i).wait_recv()

        x = xin[i].astype(F32)
        scale = lax.rsqrt(jnp.sum(x * x, axis=0, keepdims=True) * (1.0 / C) + EPS)
        scales[i] = scale
        normed = (x * scale * gain_b[...]).astype(BF)
        patches = store_patches(sp, pl.multiple_of((i + 2) * K3, 64), normed)
        conv = pre[...] + jnp.dot(weight[:, 2 * K3:], patches, preferred_element_type=F32)
        sig = 1.0 / (1.0 + jnp.exp(-conv))
        feat[i] = ((x + conv * sig) * keep(i)).astype(BF)

        @pl.when(i == 0)
        def _():
            pl.semaphore_wait(barrier, 15)

        @pl.when(seg < 3)
        def _():
            fwd_copy(i).start()

        pair_copy(i).start()
        fac[i] = sig * (1.0 + conv * (1.0 - sig))

        @pl.when(i < F - 1)
        def _():
            window = sp[pl.ds(pl.multiple_of((i + 1) * K3, 64), 2 * K3), :]
            pre[...] = jnp.dot(weight[:, :2 * K3], window, preferred_element_type=F32)

        return carry

    lax.fori_loop(0, F, forward, 0)

    @pl.when(seg == 1)
    def _():
        transpose_weight()

    @pl.when((seg == 0) & (core == 0))
    def _():
        own_weight()

    row = lax.broadcasted_iota(jnp.int32, (C, C), 0)
    colm = lax.broadcasted_iota(jnp.int32, (C, C), 1)
    blk = lax.div(row, 12)
    swapped = (lax.rem(blk, 4) * 4 + lax.div(blk, 4)) * 12 + lax.rem(row, 12)

    def z_first(h):
        return 1 - lax.rem(core + h, 2)

    def pick(h, first, second):
        return first * z_first(h) + second * (1 - z_first(h))

    def order(h):
        return jnp.where(colm == pick(h, row, swapped), 1.0, 0.0).astype(BF)

    def stage1(t, h, r):
        to = lax.rem(pick(h, zc, xc) + r, 4)
        where = {"dp": pick(h, to * 8 + xc * 2, zc * 8 + to * 2) + core}
        if h == 1:
            src, dst = c1.at[t, to], d1.at[t, r - 1]
        elif t < 2:
            src, dst = c0.at[t, to], d0.at[t, r - 1]
        else:
            src, dst = cg.at[to], dg.at[r - 1]
        return put(src, dst, s1send.at[t * 2 + h, r - 1], s1recv.at[t * 2 + h, r - 1], where)

    def emit(t, h, part):
        value = part.astype(BF)
        if t == 2 and h == 0:
            value = jnp.concatenate([value, gain_acc[...].astype(BF)], axis=1)
        rows = jnp.dot(order(h), value, preferred_element_type=F32).astype(BF)
        for q in range(4):
            if h == 1:
                c1[t, q] = rows[q * 48:(q + 1) * 48, :]
            elif t < 2:
                c0[t, q] = rows[q * 48:(q + 1) * 48, :]
            else:
                cg[q] = rows[q * 48:(q + 1) * 48, :]
        for r in (2, 1, 3):
            stage1(t, h, r).start()

    def add_columns(t):
        for acc, start, size in ((acc0, 0, N0), (acc1, N0, N1)):
            product = acc[t] * whalf[t, :, start:start + size].astype(F32)
            col_sum[:, start:start + size] += jnp.sum(product.reshape(C // 8, 8, size), axis=0)

    def gain_from_columns():
        sums = col_sum[...]
        high = sums.astype(BF)
        low = (sums - high.astype(F32)).astype(BF)
        both = jnp.concatenate([high, low], axis=0)
        per_channel = lax.dot_general(fold[...], both, NT, preferred_element_type=F32)
        gain_acc[:, 0:16] = per_channel / gain_b[:, 0:16]

    def patch_rows(t, i, start, size):
        own = pl.multiple_of((i + t) * K3 + HK * core + start, 32)
        other = pl.multiple_of((i + t) * HK + start, 32)
        return [sp[pl.ds(own, size), :], xsp[pl.ds(other, size), :]]

    def weight_product(t, frames, start, size):
        lhs, rhs = [], []
        for i in frames:
            lhs += [dc[i], odc[i]]
            rhs += patch_rows(t, i, start, size)
        return lax.dot_general(jnp.concatenate(lhs, axis=1), jnp.concatenate(rhs, axis=1), NT,
                               preferred_element_type=F32)

    pre[...] = jnp.zeros((C, PIX), F32)

    def wait_pairs():
        def body_(i, carry):
            pair_copy(i).wait_recv()
            return carry
        lax.fori_loop(0, F, body_, 0)

    @pl.when(seg == 3)
    def _():
        target.wait()

    def accumulate(t, i):
        acc0[t] += weight_product(t, [i], 0, N0)
        acc1[t] += weight_product(t, [i], N0, N1)

    def backward(n, carry):
        i = F - 1 - n

        @pl.when(seg < 3)
        def _():
            bwd_copy(i).wait_recv()

        dz = dyin[i].astype(F32) * keep(i)
        dconv = (dz * fac[i]).astype(BF)
        dc[i] = dconv
        patches = store_patches(dp_, pl.multiple_of((n + 2) * K3, 64), dconv)
        dnormed = pre[...] + jnp.dot(wt[:, 2 * K3:], patches, preferred_element_type=F32)
        x = xin[i].astype(F32)
        scale = scales[i]
        gx = dnormed * gain_b[...]
        inner = jnp.sum(gx * x, axis=0, keepdims=True)
        dx = scale * gx - x * (scale * scale * scale * inner * (1.0 / C)) + dz
        dysend[i] = dx.astype(BF)
        bwd_copy(i).start()
        dconv_copy(i).start()
        gain_acc[...] += dnormed * x * scale

        @pl.when(n < F - 1)
        def _():
            window = dp_[pl.ds(pl.multiple_of((n + 1) * K3, 64), 2 * K3), :]
            pre[...] = jnp.dot(wt[:, :2 * K3], window, preferred_element_type=F32)

        return carry

    @pl.when(seg > 0)
    def _():
        lax.fori_loop(0, F, backward, 0)
        wait_pairs()

        def arrived(i, carry):
            dconv_copy(i).wait_recv()
            return carry

        lax.fori_loop(0, F, arrived, 0)
        for t in range(3):
            frames = range(2 - t, F)
            for h in ((1, 0) if t == 2 else (0, 1)):
                emit(t, h, weight_product(t, frames, h * N0, N1 if h else N0))

    def take(n):
        i = F - 1 - n
        bwd_copy(i).wait_recv()
        dconv = (dyin[i].astype(F32) * keep(i) * fac[i]).astype(BF)
        dc[i] = dconv
        dconv_copy(i).start()

    @pl.when(seg == 0)
    def _():
        wait_pairs()
        take(0)

        def step(n, carry):
            take(n)
            i = F - n
            dconv_copy(i).wait_recv()
            for t in range(3):
                accumulate(t, i)
            return carry

        lax.fori_loop(1, F - 2, step, 0)
        take(F - 2)
        dconv_copy(2).wait_recv()
        accumulate(0, 2)
        emit(0, 0, acc0[0])
        emit(0, 1, acc1[0])
        accumulate(1, 2)
        accumulate(2, 2)
        add_columns(0)
        take(F - 1)
        dconv_copy(1).wait_recv()
        accumulate(1, 1)
        emit(1, 0, acc0[1])
        emit(1, 1, acc1[1])
        accumulate(2, 1)
        add_columns(1)
        dconv_copy(0).wait_recv()
        accumulate(2, 0)
        emit(2, 1, acc1[2])
        add_columns(2)
        gain_from_columns()
        emit(2, 0, acc0[2])

    prow = lax.broadcasted_iota(jnp.int32, (64, 48), 0)
    pcol = lax.broadcasted_iota(jnp.int32, (64, 48), 1)
    spread = jnp.where((lax.rem(prow, 8) < 6) & (pcol == lax.div(prow, 8) * 6 + lax.rem(prow, 8)), 1.0, 0.0).astype(BF)

    def stage2(h, r, c):
        to = lax.rem(pick(h, xc, zc) + r, 4)
        where = {"dp": pick(h, zc * 8 + to * 2, to * 8 + xc * 2) + c}
        slot = r * 2 + jnp.where(c == core, 0, 1)
        src, dst = ((f0, g0), (f1, g1))[h]
        return put(src.at[to * 2 + c], dst.at[core * 4 + r], s2send.at[h, slot], s2recv.at[h, slot], where)

    def collect(own, got, out, start, size):
        total = own.astype(F32)
        for r in range(3):
            total = total + got[r].astype(F32)
        spaced = jnp.dot(spread, total.astype(BF), preferred_element_type=F32).astype(BF)
        for k in range(8):
            out[k, :, start:start + size] = spaced[k * 8:(k + 1) * 8, :]

    def finish_stage1(t, h):
        for r in range(1, 4):
            stage1(t, h, r).wait_recv()
        me = pick(h, zc, xc)
        if h == 1:
            collect(c1[t, me], d1[t], f1, t * N1, N1)
        elif t < 2:
            collect(c0[t, me], d0[t], f0, t * N0, N0)
        else:
            collect(cg[me], dg[...], f0, 2 * N0, N0 + PIX)

    def settle(i, carry):
        pair_copy(i).wait_send()
        dconv_copy(i).wait_send()

        @pl.when(seg < 3)
        def _():
            fwd_copy(i).wait_send()

        @pl.when(seg > 0)
        def _():
            bwd_copy(i).wait_send()

        return carry

    for t in range(2):
        for h in range(2):
            finish_stage1(t, h)
    lax.fori_loop(0, F, settle, 0)
    for h in (1, 0):
        finish_stage1(2, h)
        for r in (2, 1, 3):
            stage2(h, r, core).start()
            stage2(h, r, 1 - core).start()
        stage2(h, 0, 1 - core).start()

    for r in range(1, 4):
        for t in range(3):
            stage1(t, 0, r).wait_send()
            stage1(t, 1, r).wait_send()

    def stage2_wait(h, r, c):
        slot = r * 2 + jnp.where(c == core, 0, 1)
        src, dst = ((f0, g0), (f1, g1))[h]
        return put(src.at[0], dst.at[c * 4 + r], s2send.at[h, slot], s2recv.at[h, slot], dev(zc, xc, 1 - core))

    for h in (1, 0):
        src, dst = ((f0, g0), (f1, g1))[h]
        dst[core * 4] = src[pick(h, xc, zc) * 2 + core]
        for r in range(4):
            if r:
                stage2_wait(h, r, core).wait_recv()
            stage2_wait(h, r, 1 - core).wait_recv()
        for c in range(2):
            total = dst[c * 4].astype(F32)
            for r in range(1, 4):
                total = total + dst[c * 4 + r].astype(F32)
            if h == 0:
                per_row = jnp.sum(total[:, 3 * N0:], axis=1, keepdims=True)
                gain_rows = per_row if c == 0 else gain_rows + per_row
            for t in range(3):
                start = t * K3 + c * HK + (0 if h == 0 else N0)
                size = N0 if h == 0 else HK - N0
                first = t * (N0 if h == 0 else N1)
                for j in range(6):
                    dweight[j, :, start:start + size] = total[j:j + 1, first:first + size]

    r8 = lax.broadcasted_iota(jnp.int32, (8, 128), 0)
    l8 = lax.broadcasted_iota(jnp.int32, (8, 128), 1)
    dgain[...] = jnp.sum(jnp.where(r8 == l8, gain_rows, 0.0), axis=0, keepdims=True)

    for h in range(2):
        for r in range(4):
            if r:
                stage2_wait(h, r, core).wait_send()
            stage2_wait(h, r, 1 - core).wait_send()


def hand_over(feat, dweight, dgain, feat_out, dweight_out, dgain_out, sems):
    copies = (pltpu.make_async_copy(feat, feat_out, sems.at[0]),
              pltpu.make_async_copy(dweight, dweight_out, sems.at[1]))
    for copy in copies:
        copy.start()
    dgain_out[...] = dgain[:, 0:6]
    for copy in copies:
        copy.wait()


def body(video_clips, conv_weight, norm_gain, cotangent, clip_groups):
    vmem = pl.BlockSpec(memory_space=pltpu.VMEM)
    hbm = pl.BlockSpec(memory_space=pl.ANY)
    dma = pltpu.SemaphoreType.DMA
    feat, dweight, dgain = pl.pallas_call(
        kernel,
        out_shape=(
            jax.ShapeDtypeStruct((F, C, PIX), BF),
            jax.ShapeDtypeStruct((6, 1, KK), F32),
            jax.ShapeDtypeStruct((1, 128), F32),
        ),
        in_specs=[vmem, hbm, hbm, hbm, hbm],
        out_specs=(vmem, vmem, vmem),
        scratch_shapes=[
            pltpu.VMEM((1, C), F32),
            pltpu.VMEM((C, KK), BF),
            pltpu.VMEM((F, C, PIX), BF),
            pltpu.VMEM((C, PIX), F32),
            pltpu.VMEM((F, C, PIX), BF),
            pltpu.VMEM((F, C, PIX), BF),
            pltpu.VMEM((F, C, PIX), BF),
            pltpu.VMEM((F, C, PIX), F32),
            pltpu.VMEM((F, 1, PIX), F32),
            pltpu.VMEM((C, PIX), F32),
            pltpu.VMEM((C, PIX), F32),
            pltpu.VMEM((11 * K3 + 32, PIX), BF),
            pltpu.VMEM((11 * HK + 32, PIX), BF),
            pltpu.VMEM((11 * K3, PIX), BF),
            pltpu.VMEM((C, KK), BF),
            pltpu.VMEM((3, C, N0 + N1), BF),
            pltpu.VMEM((C, N0 + N1), BF),
            pltpu.VMEM((F, C, PIX), BF),
            pltpu.VMEM((F, C, PIX), BF),
            pltpu.VMEM((3, C, N0), F32),
            pltpu.VMEM((3, C, N1), F32),
            pltpu.VMEM((8, N0 + N1), F32),
            pltpu.VMEM((2, 4, 48, N0), BF),
            pltpu.VMEM((3, 4, 48, N1), BF),
            pltpu.VMEM((4, 48, N0 + PIX), BF),
            pltpu.VMEM((2, 3, 48, N0), BF),
            pltpu.VMEM((3, 3, 48, N1), BF),
            pltpu.VMEM((3, 48, N0 + PIX), BF),
            pltpu.VMEM((8, 8, 3 * N0 + PIX), BF),
            pltpu.VMEM((8, 8, 3 * N1), BF),
            pltpu.VMEM((8, 8, 3 * N0 + PIX), BF),
            pltpu.VMEM((8, 8, 3 * N1), BF),
            dma((4,)),
            dma((F,)), dma((F,)), dma((F,)), dma((F,)),
            dma((F,)), dma((F,)), dma((F,)), dma((F,)),
            dma((6, 3)), dma((6, 3)),
            dma((2, 8)), dma((2, 8)),
        ],
        compiler_params=pltpu.CompilerParams(
            collective_id=0, has_side_effects=True, vmem_limit_bytes=36 << 20),
    )(clip_groups, *(pltpu.with_memory_space_constraint(v, pltpu.HBM) for v in (video_clips[0], conv_weight[0])), pltpu.with_memory_space_constraint(norm_gain, pltpu.HBM), pltpu.with_memory_space_constraint(cotangent[0], pltpu.HBM))
    feat, dweight, dgain = pl.pallas_call(
        hand_over,
        out_shape=(
            jax.ShapeDtypeStruct((F, C, PIX), BF),
            jax.ShapeDtypeStruct((6, 1, KK), F32),
            jax.ShapeDtypeStruct((1, 6), F32),
        ),
        in_specs=[hbm, hbm, vmem],
        out_specs=(hbm, hbm, vmem),
        scratch_shapes=[dma((2,))],
        compiler_params=pltpu.CompilerParams(vmem_limit_bytes=4 << 20),
    )(feat, dweight, dgain)
    return (feat[None, None], jnp.transpose(dweight, (1, 0, 2)), dgain)


def solution(mesh):
    placed = (
        P("dp", None, None, None),
        P("segment", None, None),
        P("segment", None),
        P("dp", None, None, None),
        P("dp"),
    )
    return jax.shard_map(
        body,
        mesh=mesh,
        in_specs=placed,
        out_specs=(
            P("segment", "dp", None, None, None),
            P("segment", "dp", None),
            P("segment", "dp"),
        ),
        check_vma=False,
    )
```

```python
import jax
import jax.numpy as jnp
from jax import lax
from jax.experimental import pallas as pl
from jax.experimental.pallas import tpu as pltpu
from jax.sharding import PartitionSpec as P

TILE_H = 8
TILE_W = 16
EPS = 1e-06

F = 9
C = 192
PIX = 128
K3 = 9 * C
KK = 27 * C
HK = K3 // 2
N0 = 512
N1 = 384

BF = jnp.bfloat16
F32 = jnp.float32
NT = (((1,), (1,)), ((), ()))


def tap_masks():
    lane = lax.broadcasted_iota(jnp.int32, (1, PIX), 1)
    col = lane & (TILE_W - 1)
    masks = []
    for a in range(3):
        for b in range(3):
            pos = lane + TILE_W * (a - 1)
            ok = (col + (b - 1) >= 0) & (col + (b - 1) < TILE_W) & (pos >= 0) & (pos < PIX)
            masks.append(jnp.where(ok, 1.0, 0.0).astype(BF))
    return masks


def store_patches(dst, base, frame):
    masks = tap_masks()
    values = []
    for a in range(3):
        for b in range(3):
            k = a * 3 + b
            shift = (-(TILE_W * (a - 1) + (b - 1))) % PIX
            values.append(frame if shift == 0 else pltpu.roll(frame, shift, 1) * masks[k])
    patches = jnp.concatenate(values, axis=0)
    dst[pl.ds(base, K3), :] = patches
    return patches


def kernel(groups, video, weight_hbm, gain_hbm, cot, feat, dweight, dgain,
           gain, weight, video_v, pre, xin, dyin, dysend, fac, scales, gain_b, gain_acc,
           sp, xsp, dp_, wt, whalf, fold, dc, odc, acc0, acc1, col_sum,
           c0, c1, cg, d0, d1, dg, f0, f1, g0, g1,
           insem, fsend, frecv, bsend, brecv, psend, precv, csend, crecv,
           s1send, s1recv, s2send, s2recv):
    seg = lax.axis_index("segment")
    d = lax.axis_index("dp")
    core = lax.rem(d, 2)
    xc = lax.rem(lax.div(d, 2), 4)
    zc = lax.div(d, 8)

    def dev(z, x, c):
        return {"dp": (z * 4 + x) * 2 + c}

    def put(src, dst, ssem, rsem, where):
        return pltpu.make_async_remote_copy(
            src_ref=src, dst_ref=dst, send_sem=ssem, recv_sem=rsem,
            device_id=where, device_id_type=pl.DeviceIdType.MESH)

    barrier = pltpu.get_barrier_semaphore()

    def greet(where):
        pl.semaphore_signal(barrier, inc=1, device_id=where, device_id_type=pl.DeviceIdType.MESH)

    greet({"segment": lax.rem(seg + 1, 4)})
    greet({"segment": lax.rem(seg + 3, 4)})
    greet(dev(zc, xc, 1 - core))
    for r in range(1, 4):
        for c in range(2):
            greet(dev(lax.rem(zc + r, 4), xc, c))
            greet(dev(zc, lax.rem(xc + r, 4), c))

    early = pltpu.make_async_copy(weight_hbm.at[:, 2 * K3:], weight.at[:, 2 * K3:], insem.at[0])
    late = pltpu.make_async_copy(weight_hbm.at[:, :2 * K3], weight.at[:, :2 * K3], insem.at[1])
    clip = pltpu.make_async_copy(video, video_v, insem.at[2])
    target = pltpu.make_async_copy(cot, dyin, insem.at[2])

    @pl.when(seg == 0)
    def _():
        clip.start()

    gains = pltpu.make_async_copy(gain_hbm, gain, insem.at[3])
    gains.start()
    early.start()
    late.start()

    @pl.when(seg == 3)
    def _():
        target.start()

    count = groups[...].reshape(1, 1) * 4 - 3

    def keep(i):
        return jnp.where(i < count, 1.0, 0.0).astype(F32)

    zero_patch = jnp.zeros((K3, PIX), BF)
    sp[0:K3, :] = zero_patch
    sp[K3:2 * K3, :] = zero_patch
    sp[11 * K3:, :] = jnp.zeros((32, PIX), BF)
    xsp[0:K3, :] = zero_patch
    xsp[11 * HK:, :] = jnp.zeros((32, PIX), BF)
    dp_[0:K3, :] = zero_patch
    dp_[K3:2 * K3, :] = zero_patch
    pre[...] = jnp.zeros((C, PIX), F32)
    gains.wait()
    gain_b[...] = jnp.broadcast_to(gain[...], (PIX, C)).T
    gain_acc[...] = jnp.zeros((C, PIX), F32)
    col_sum[...] = jnp.zeros((8, N0 + N1), F32)
    acc0[...] = jnp.zeros((3, C, N0), F32)
    acc1[...] = jnp.zeros((3, C, N1), F32)

    def transpose_weight():
        for tap in range(27):
            to = (tap // 9) * 9 + 8 - tap % 9
            wt[:, to * C:(to + 1) * C] = weight[:, tap * C:(tap + 1) * C].T

    def own_weight():
        for t in range(3):
            for c in range(2):
                @pl.when(core == c)
                def _():
                    start = t * K3 + c * HK
                    whalf[t, :, 0:HK] = weight[:, start:start + HK]

            whalf[t, :, HK:] = jnp.zeros((C, N0 + N1 - HK), BF)
        lane = lax.broadcasted_iota(jnp.int32, (C, N0 + N1), 1) + HK * core
        channel = lax.broadcasted_iota(jnp.int32, (C, N0 + N1), 0)
        fold[...] = jnp.where(lax.rem(lane, C) == channel, 1.0, 0.0).astype(BF)

    @pl.when(seg == 0)
    def _():
        clip.wait()
        for i in range(F):
            xin[i] = (video_v[i].astype(F32) * keep(i)).astype(BF)

    early.wait()
    late.wait()

    @pl.when((seg == 0) & (core == 1))
    def _():
        own_weight()

    @pl.when(seg >= 2)
    def _():
        transpose_weight()

    def fwd_copy(i):
        return put(feat.at[i], xin.at[i], fsend.at[i], frecv.at[i], {"segment": lax.rem(seg + 1, 4)})

    def bwd_copy(i):
        return put(dysend.at[i], dyin.at[i], bsend.at[i], brecv.at[i], {"segment": lax.rem(seg + 3, 4)})

    def pair_copy(i):
        src = pl.multiple_of((i + 2) * K3 + HK * (1 - core), 32)
        dst = pl.multiple_of((i + 2) * HK, 32)
        return put(sp.at[pl.ds(src, HK), :], xsp.at[pl.ds(dst, HK), :], psend.at[i], precv.at[i], dev(zc, xc, 1 - core))

    def dconv_copy(i):
        return put(dc.at[i], odc.at[i], csend.at[i], crecv.at[i], dev(zc, xc, 1 - core))

    def forward(i, carry):
        @pl.when(seg > 0)
        def _():
            fwd_copy(i).wait_recv()

        x = xin[i].astype(F32)
        scale = lax.rsqrt(jnp.sum(x * x, axis=0, keepdims=True) * (1.0 / C) + EPS)
        scales[i] = scale
        normed = (x * scale * gain_b[...]).astype(BF)
        patches = store_patches(sp, pl.multiple_of((i + 2) * K3, 64), normed)
        conv = pre[...] + jnp.dot(weight[:, 2 * K3:], patches, preferred_element_type=F32)
        sig = 1.0 / (1.0 + jnp.exp(-conv))
        feat[i] = ((x + conv * sig) * keep(i)).astype(BF)

        @pl.when(i == 0)
        def _():
            pl.semaphore_wait(barrier, 15)

        @pl.when(seg < 3)
        def _():
            fwd_copy(i).start()

        pair_copy(i).start()
        fac[i] = sig * (1.0 + conv * (1.0 - sig))

        @pl.when(i < F - 1)
        def _():
            window = sp[pl.ds(pl.multiple_of((i + 1) * K3, 64), 2 * K3), :]
            pre[...] = jnp.dot(weight[:, :2 * K3], window, preferred_element_type=F32)

        return carry

    lax.fori_loop(0, F, forward, 0)

    @pl.when(seg == 1)
    def _():
        transpose_weight()

    @pl.when((seg == 0) & (core == 0))
    def _():
        own_weight()

    row = lax.broadcasted_iota(jnp.int32, (C, C), 0)
    colm = lax.broadcasted_iota(jnp.int32, (C, C), 1)
    blk = lax.div(row, 12)
    swapped = (lax.rem(blk, 4) * 4 + lax.div(blk, 4)) * 12 + lax.rem(row, 12)

    def z_first(h):
        return 1 - lax.rem(core + h, 2)

    def pick(h, first, second):
        return first * z_first(h) + second * (1 - z_first(h))

    def order(h):
        return jnp.where(colm == pick(h, row, swapped), 1.0, 0.0).astype(BF)

    def stage1(t, h, r):
        to = lax.rem(pick(h, zc, xc) + r, 4)
        where = {"dp": pick(h, to * 8 + xc * 2, zc * 8 + to * 2) + core}
        if h == 1:
            src, dst = c1.at[t, to], d1.at[t, r - 1]
        elif t < 2:
            src, dst = c0.at[t, to], d0.at[t, r - 1]
        else:
            src, dst = cg.at[to], dg.at[r - 1]
        return put(src, dst, s1send.at[t * 2 + h, r - 1], s1recv.at[t * 2 + h, r - 1], where)

    def emit(t, h, part):
        value = part.astype(BF)
        if t == 2 and h == 0:
            value = jnp.concatenate([value, gain_acc[...].astype(BF)], axis=1)

        def place(rows):
            for q in range(4):
                block = rows[q * 48:(q + 1) * 48, :]
                if h == 1:
                    c1[t, q] = block
                elif t < 2:
                    c0[t, q] = block
                else:
                    cg[q] = block

        @pl.when(z_first(h) == 1)
        def _():
            place(value)

        @pl.when(z_first(h) == 0)
        def _():
            place(jnp.dot(order(h), value, preferred_element_type=F32).astype(BF))

        for r in (2, 1, 3):
            stage1(t, h, r).start()

    def add_columns(t):
        for acc, start, size in ((acc0, 0, N0), (acc1, N0, N1)):
            product = acc[t] * whalf[t, :, start:start + size].astype(F32)
            col_sum[:, start:start + size] += jnp.sum(product.reshape(C // 8, 8, size), axis=0)

    def gain_from_columns():
        sums = col_sum[...]
        high = sums.astype(BF)
        low = (sums - high.astype(F32)).astype(BF)
        both = jnp.concatenate([high, low], axis=0)
        per_channel = lax.dot_general(fold[...], both, NT, preferred_element_type=F32)
        gain_acc[:, 0:16] = per_channel / gain_b[:, 0:16]

    def patch_rows(t, i, start, size):
        own = pl.multiple_of((i + t) * K3 + HK * core + start, 32)
        other = pl.multiple_of((i + t) * HK + start, 32)
        return [sp[pl.ds(own, size), :], xsp[pl.ds(other, size), :]]

    def weight_product(t, frames, start, size):
        lhs, rhs = [], []
        for i in frames:
            lhs += [dc[i], odc[i]]
            rhs += patch_rows(t, i, start, size)
        return lax.dot_general(jnp.concatenate(lhs, axis=1), jnp.concatenate(rhs, axis=1), NT,
                               preferred_element_type=F32)

    pre[...] = jnp.zeros((C, PIX), F32)

    def wait_pairs():
        def body_(i, carry):
            pair_copy(i).wait_recv()
            return carry
        lax.fori_loop(0, F, body_, 0)

    @pl.when(seg == 3)
    def _():
        target.wait()

    def accumulate(t, i):
        acc0[t] += weight_product(t, [i], 0, N0)
        acc1[t] += weight_product(t, [i], N0, N1)

    def backward(n, carry):
        i = F - 1 - n

        @pl.when(seg < 3)
        def _():
            bwd_copy(i).wait_recv()

        dz = dyin[i].astype(F32) * keep(i)
        dconv = (dz * fac[i]).astype(BF)
        dc[i] = dconv
        patches = store_patches(dp_, pl.multiple_of((n + 2) * K3, 64), dconv)
        dnormed = pre[...] + jnp.dot(wt[:, 2 * K3:], patches, preferred_element_type=F32)
        x = xin[i].astype(F32)
        scale = scales[i]
        gx = dnormed * gain_b[...]
        inner = jnp.sum(gx * x, axis=0, keepdims=True)
        dx = scale * gx - x * (scale * scale * scale * inner * (1.0 / C)) + dz
        dysend[i] = dx.astype(BF)
        bwd_copy(i).start()
        dconv_copy(i).start()
        gain_acc[...] += dnormed * x * scale

        @pl.when(n < F - 1)
        def _():
            window = dp_[pl.ds(pl.multiple_of((n + 1) * K3, 64), 2 * K3), :]
            pre[...] = jnp.dot(wt[:, :2 * K3], window, preferred_element_type=F32)

        return carry

    @pl.when(seg > 0)
    def _():
        lax.fori_loop(0, F, backward, 0)
        wait_pairs()

        def arrived(i, carry):
            dconv_copy(i).wait_recv()
            return carry

        lax.fori_loop(0, F, arrived, 0)
        for t in range(3):
            frames = range(2 - t, F)
            for h in ((1, 0) if t == 2 else (0, 1)):
                emit(t, h, weight_product(t, frames, h * N0, N1 if h else N0))

    def take(n):
        i = F - 1 - n
        bwd_copy(i).wait_recv()
        dconv = (dyin[i].astype(F32) * keep(i) * fac[i]).astype(BF)
        dc[i] = dconv
        dconv_copy(i).start()

    @pl.when(seg == 0)
    def _():
        wait_pairs()
        take(0)

        def step(n, carry):
            take(n)
            i = F - n
            dconv_copy(i).wait_recv()
            for t in range(3):
                accumulate(t, i)
            return carry

        lax.fori_loop(1, F - 2, step, 0)
        take(F - 2)
        dconv_copy(2).wait_recv()
        accumulate(0, 2)
        emit(0, 0, acc0[0])
        emit(0, 1, acc1[0])
        accumulate(1, 2)
        accumulate(2, 2)
        add_columns(0)
        take(F - 1)
        dconv_copy(1).wait_recv()
        accumulate(1, 1)
        emit(1, 0, acc0[1])
        emit(1, 1, acc1[1])
        accumulate(2, 1)
        add_columns(1)
        dconv_copy(0).wait_recv()
        accumulate(2, 0)
        emit(2, 1, acc1[2])
        add_columns(2)
        gain_from_columns()
        emit(2, 0, acc0[2])

    prow = lax.broadcasted_iota(jnp.int32, (64, 48), 0)
    pcol = lax.broadcasted_iota(jnp.int32, (64, 48), 1)
    spread = jnp.where((lax.rem(prow, 8) < 6) & (pcol == lax.div(prow, 8) * 6 + lax.rem(prow, 8)), 1.0, 0.0).astype(BF)

    def stage2(h, r, c):
        to = lax.rem(pick(h, xc, zc) + r, 4)
        where = {"dp": pick(h, zc * 8 + to * 2, to * 8 + xc * 2) + c}
        slot = r * 2 + jnp.where(c == core, 0, 1)
        src, dst = ((f0, g0), (f1, g1))[h]
        return put(src.at[to * 2 + c], dst.at[core * 4 + r], s2send.at[h, slot], s2recv.at[h, slot], where)

    def collect(own, got, out, start, size):
        total = own.astype(F32)
        for r in range(3):
            total = total + got[r].astype(F32)
        spaced = jnp.dot(spread, total.astype(BF), preferred_element_type=F32).astype(BF)
        for k in range(8):
            out[k, :, start:start + size] = spaced[k * 8:(k + 1) * 8, :]

    def finish_stage1(t, h):
        for r in range(1, 4):
            stage1(t, h, r).wait_recv()
        me = pick(h, zc, xc)
        if h == 1:
            collect(c1[t, me], d1[t], f1, t * N1, N1)
        elif t < 2:
            collect(c0[t, me], d0[t], f0, t * N0, N0)
        else:
            collect(cg[me], dg[...], f0, 2 * N0, N0 + PIX)

    def settle(i, carry):
        pair_copy(i).wait_send()
        dconv_copy(i).wait_send()

        @pl.when(seg < 3)
        def _():
            fwd_copy(i).wait_send()

        @pl.when(seg > 0)
        def _():
            bwd_copy(i).wait_send()

        return carry

    for t in range(2):
        for h in range(2):
            finish_stage1(t, h)
    lax.fori_loop(0, F, settle, 0)
    for h in (1, 0):
        finish_stage1(2, h)
        for r in (2, 1, 3):
            stage2(h, r, core).start()
            stage2(h, r, 1 - core).start()
        stage2(h, 0, 1 - core).start()

    for r in range(1, 4):
        for t in range(3):
            stage1(t, 0, r).wait_send()
            stage1(t, 1, r).wait_send()

    def stage2_wait(h, r, c):
        slot = r * 2 + jnp.where(c == core, 0, 1)
        src, dst = ((f0, g0), (f1, g1))[h]
        return put(src.at[0], dst.at[c * 4 + r], s2send.at[h, slot], s2recv.at[h, slot], dev(zc, xc, 1 - core))

    for h in (1, 0):
        src, dst = ((f0, g0), (f1, g1))[h]
        dst[core * 4] = src[pick(h, xc, zc) * 2 + core]
        for r in range(4):
            if r:
                stage2_wait(h, r, core).wait_recv()
            stage2_wait(h, r, 1 - core).wait_recv()
        for c in range(2):
            total = dst[c * 4].astype(F32)
            for r in range(1, 4):
                total = total + dst[c * 4 + r].astype(F32)
            if h == 0:
                per_row = jnp.sum(total[:, 3 * N0:], axis=1, keepdims=True)
                gain_rows = per_row if c == 0 else gain_rows + per_row
            for t in range(3):
                start = t * K3 + c * HK + (0 if h == 0 else N0)
                size = N0 if h == 0 else HK - N0
                first = t * (N0 if h == 0 else N1)
                for j in range(6):
                    dweight[j, :, start:start + size] = total[j:j + 1, first:first + size]

    r8 = lax.broadcasted_iota(jnp.int32, (8, 128), 0)
    l8 = lax.broadcasted_iota(jnp.int32, (8, 128), 1)
    dgain[...] = jnp.sum(jnp.where(r8 == l8, gain_rows, 0.0), axis=0, keepdims=True)

    for h in range(2):
        for r in range(4):
            if r:
                stage2_wait(h, r, core).wait_send()
            stage2_wait(h, r, 1 - core).wait_send()


def hand_over(feat, dweight, dgain, feat_out, dweight_out, dgain_out, sems):
    copies = (pltpu.make_async_copy(feat, feat_out, sems.at[0]),
              pltpu.make_async_copy(dweight, dweight_out, sems.at[1]))
    for copy in copies:
        copy.start()
    dgain_out[...] = dgain[:, 0:6]
    for copy in copies:
        copy.wait()


def body(video_clips, conv_weight, norm_gain, cotangent, clip_groups):
    vmem = pl.BlockSpec(memory_space=pltpu.VMEM)
    hbm = pl.BlockSpec(memory_space=pl.ANY)
    dma = pltpu.SemaphoreType.DMA
    feat, dweight, dgain = pl.pallas_call(
        kernel,
        out_shape=(
            jax.ShapeDtypeStruct((F, C, PIX), BF),
            jax.ShapeDtypeStruct((6, 1, KK), F32),
            jax.ShapeDtypeStruct((1, 128), F32),
        ),
        in_specs=[vmem, hbm, hbm, hbm, hbm],
        out_specs=(vmem, vmem, vmem),
        scratch_shapes=[
            pltpu.VMEM((1, C), F32),
            pltpu.VMEM((C, KK), BF),
            pltpu.VMEM((F, C, PIX), BF),
            pltpu.VMEM((C, PIX), F32),
            pltpu.VMEM((F, C, PIX), BF),
            pltpu.VMEM((F, C, PIX), BF),
            pltpu.VMEM((F, C, PIX), BF),
            pltpu.VMEM((F, C, PIX), F32),
            pltpu.VMEM((F, 1, PIX), F32),
            pltpu.VMEM((C, PIX), F32),
            pltpu.VMEM((C, PIX), F32),
            pltpu.VMEM((11 * K3 + 32, PIX), BF),
            pltpu.VMEM((11 * HK + 32, PIX), BF),
            pltpu.VMEM((11 * K3, PIX), BF),
            pltpu.VMEM((C, KK), BF),
            pltpu.VMEM((3, C, N0 + N1), BF),
            pltpu.VMEM((C, N0 + N1), BF),
            pltpu.VMEM((F, C, PIX), BF),
            pltpu.VMEM((F, C, PIX), BF),
            pltpu.VMEM((3, C, N0), F32),
            pltpu.VMEM((3, C, N1), F32),
            pltpu.VMEM((8, N0 + N1), F32),
            pltpu.VMEM((2, 4, 48, N0), BF),
            pltpu.VMEM((3, 4, 48, N1), BF),
            pltpu.VMEM((4, 48, N0 + PIX), BF),
            pltpu.VMEM((2, 3, 48, N0), BF),
            pltpu.VMEM((3, 3, 48, N1), BF),
            pltpu.VMEM((3, 48, N0 + PIX), BF),
            pltpu.VMEM((8, 8, 3 * N0 + PIX), BF),
            pltpu.VMEM((8, 8, 3 * N1), BF),
            pltpu.VMEM((8, 8, 3 * N0 + PIX), BF),
            pltpu.VMEM((8, 8, 3 * N1), BF),
            dma((4,)),
            dma((F,)), dma((F,)), dma((F,)), dma((F,)),
            dma((F,)), dma((F,)), dma((F,)), dma((F,)),
            dma((6, 3)), dma((6, 3)),
            dma((2, 8)), dma((2, 8)),
        ],
        compiler_params=pltpu.CompilerParams(
            collective_id=0, has_side_effects=True, vmem_limit_bytes=36 << 20),
    )(clip_groups, *(pltpu.with_memory_space_constraint(v, pltpu.HBM) for v in (video_clips[0], conv_weight[0])), pltpu.with_memory_space_constraint(norm_gain, pltpu.HBM), pltpu.with_memory_space_constraint(cotangent[0], pltpu.HBM))
    feat, dweight, dgain = pl.pallas_call(
        hand_over,
        out_shape=(
            jax.ShapeDtypeStruct((F, C, PIX), BF),
            jax.ShapeDtypeStruct((6, 1, KK), F32),
            jax.ShapeDtypeStruct((1, 6), F32),
        ),
        in_specs=[hbm, hbm, vmem],
        out_specs=(hbm, hbm, vmem),
        scratch_shapes=[dma((2,))],
        compiler_params=pltpu.CompilerParams(vmem_limit_bytes=4 << 20),
    )(feat, dweight, dgain)
    return (feat[None, None], jnp.transpose(dweight, (1, 0, 2)), dgain)


def solution(mesh):
    placed = (
        P("dp", None, None, None),
        P("segment", None, None),
        P("segment", None),
        P("dp", None, None, None),
        P("dp"),
    )
    return jax.shard_map(
        body,
        mesh=mesh,
        in_specs=placed,
        out_specs=(
            P("segment", "dp", None, None, None),
            P("segment", "dp", None),
            P("segment", "dp"),
        ),
        check_vma=False,
    )
```
